512 devices in a mesh: shard: 32 (over y_lo, z), rep: 16 (over x, y_hi, core).
Axes of the slice: x: 4, y: 4 (y_hi: 2, y_lo: 2; y = y_hi * 2 + y_lo), z: 16, core: 2. Of those that a mesh axis runs over, the one named last changes fastest.
Arguments:
- node_feat: bfloat16 [4096, 128, 256], P(('shard', 'rep'))
- node_cot: bfloat16 [4096, 128, 256], P(('shard', 'rep'))
- edge_length: float32 [4096, 1536], P(('shard', 'rep')), may hold values from 0.5 to 5.5
- atom_count: int32 [4096], P(('shard', 'rep')), may hold values from 32 to 128, as said below
- edge_count: int32 [4096], P(('shard', 'rep')), may hold values from 384 to 1536, as said below
- edge_source: int32 [4096, 1536], P(('shard', 'rep')), may hold values from 0 to 127, as said below
- edge_target: int32 [4096, 1536], P(('shard', 'rep')), may hold values from 0 to 127, as said below
- dataset_tag: int32 [4096], P(('shard', 'rep')), may hold values from 0 to 1
- charge_tag: int32 [4096], P(('shard', 'rep')), may hold values from 0 to 1
- spin_tag: int32 [4096], P(('shard', 'rep')), may hold values from 0 to 1
- dataset_gain: float32 [2, 32], replicated, may hold values from 0.2 to 5
- charge_gain: float32 [2, 32], replicated, may hold values from 0.2 to 5
- spin_gain: float32 [2, 32], replicated, may hold values from 0.2 to 5
- params: float32 [32, 128, 2, 128], P(None, 'shard'), may hold values from -0.375 to 0.375
- moment_one: float32 [32, 128, 2, 128], P(None, 'shard'), may hold values from -0.9 to 0.9
- moment_two: float32 [32, 128, 2, 128], P(None, 'shard'), may hold values from 0.0001 to 0.01
Outputs:
- new_params: float32 [32, 128, 2, 128], P(None, 'shard')
- new_moment_one: float32 [32, 128, 2, 128], P(None, 'shard')
- new_moment_two: float32 [32, 128, 2, 128], P(None, 'shard')
- full_weights: bfloat16 [32, 128, 2, 128], replicated
The draws below stay inside these ranges and needn't reach their ends.
Inputs may be any that keep to these rules, and one draw needn't show every extreme that they name: `atom_count`: every system has at least a quarter of its atom slots filled. `edge_count`: every system has at least a quarter of its edge slots live. `edge_source`: every slot, live or not, names an atom below its system's atom count. `edge_target`: every slot, live or not, names an atom below its system's atom count.
All inputs are finite; a program needn't handle non-finite values.
Results may differ from the reference program's by a relative error of at most 0.0036.
Values may be sent and summed in bfloat16 or wider, within the bound.
No kernel may reach another device: no remote copies, remote signals or barrier semaphores. Data moves between devices by JAX's collectives and lax.ppermute only.
A program may use at most 64 MiB of HBM per device.

```python
import math
import jax
import jax.numpy as jnp
from jax import lax

CH = 128
EXPERTS = 32
DATASETS = 2
CHARGES = 2
SPINS = 2
ATOMS = 128
EDGE_SLOTS = 1536
STEP = 10
SYS_DEV = 8
SYSTEMS = 4096


def system_atoms(key):
    counts_key = jax.random.fold_in(key, 101)
    counts = jax.random.randint(counts_key, (SYSTEMS,), ATOMS // 4, ATOMS + 1)
    counts = counts.at[::SYS_DEV].set(ATOMS)
    return counts.astype(jnp.int32)


def edge_atoms(key, salt):
    counts = system_atoms(key)
    raw_key = jax.random.fold_in(key, salt)
    raw_draw = jax.random.randint(raw_key, (SYSTEMS, EDGE_SLOTS), 0, 1073741824)
    chosen = raw_draw % counts[:, None]
    chosen = chosen.at[::SYS_DEV, 0].set(ATOMS - 1)
    return chosen.astype(jnp.int32)


def draw_atom_count(key, part):
    return system_atoms(key)


def draw_edge_count(key, part):
    count_key = jax.random.fold_in(key, 202)
    counts = jax.random.randint(count_key, (SYSTEMS,), EDGE_SLOTS // 4, EDGE_SLOTS + 1)
    counts = counts.at[::SYS_DEV].set(EDGE_SLOTS)
    return counts.astype(jnp.int32)


def draw_edge_source(key, part):
    return edge_atoms(key, 303)


def draw_edge_target(key, part):
    return edge_atoms(key, 404)


def draw_node_feat(key, part):
    value_key = jax.random.fold_in(key, 505)
    row_key = jax.random.fold_in(key, 606)
    column_key = jax.random.fold_in(key, 707)
    pattern_key = jax.random.fold_in(key, 808)
    shared_key = jax.random.fold_in(key, 909)
    sign_key = jax.random.fold_in(key, 1010)
    channel = jnp.arange(2 * CH) % CH
    trend = channel.astype(jnp.float32) / float(max(CH - 1, 1))
    column_draw = jax.random.uniform(column_key, (CH,), jnp.float32)
    column_scale = 10.0 ** (0.5 * trend + 0.5 * column_draw[channel])
    row_scale = 10.0 ** jax.random.uniform(row_key, (SYSTEMS, ATOMS, 1), jnp.float32)
    pattern = jax.random.normal(pattern_key, (1, 1, 2 * CH), jnp.float32)
    shared = jax.random.normal(shared_key, (1, 1, 2 * CH), jnp.float32)
    signs = (jax.random.randint(sign_key, (SYSTEMS, 1, 1), 0, 2) * 2 - 1).astype(jnp.float32)
    shared_weight = float(SYSTEMS) ** (-0.5)
    base = jax.random.normal(value_key, (SYSTEMS, ATOMS, 2 * CH), jnp.float32)
    offset = 0.8 * (signs * pattern + shared_weight * shared)
    return ((base + offset) * column_scale[None, None, :] * row_scale).astype(jnp.bfloat16)


def draw_node_cot(key, part):
    value_key = jax.random.fold_in(key, 1111)
    mean_key = jax.random.fold_in(key, 1212)
    column_mean = jax.random.normal(mean_key, (1, 1, 2 * CH), jnp.float32)
    base = jax.random.normal(value_key, (SYSTEMS, ATOMS, 2 * CH), jnp.float32)
    values = base + 0.3 * column_mean
    return jnp.clip(values, -6.0, 6.0).astype(jnp.bfloat16)


def touch_ends(result, own_key, smallest, largest):
    spot = [jax.random.randint(jax.random.fold_in(own_key, axis), (), 0, length) for axis, length in enumerate(result.shape)]
    main_axis = result.shape.index(max(result.shape))
    neighbour = spot[:main_axis] + [(spot[main_axis] + 1) % result.shape[main_axis]] + spot[main_axis + 1:]
    return result.at[tuple(spot)].set(smallest).at[tuple(neighbour)].set(largest)


def level_of(key, shape, shards, least, high):
    factor_of = 1.0
    for axis_at, shards_of in shards:
        draws = jax.random.uniform(jax.random.fold_in(jax.random.fold_in(key, 6), axis_at), (shards_of,), jnp.float32, least / len(shards), high / len(shards))
        factor_of = factor_of * jnp.repeat(jnp.exp(draws), shape[axis_at] // shards_of).reshape((-1,) + (1,) * (len(shape) - 1 - axis_at))
    return factor_of


def centred(stream_key, extent, scale, bound, pieces=(), held_as=jnp.bfloat16):
    drawn = jax.random.normal(stream_key, extent, jnp.float32) * scale
    if len(pieces) > 0:
        drawn = level_of(stream_key, extent, pieces, -0.22, 0.18) * drawn
    return jnp.clip(drawn, min=-bound, max=bound).astype(held_as)


def setup_inputs(seed: int = 0) -> dict:
    splits = jax.random.split(jax.random.key(seed), 17)
    node_feat = draw_node_feat(jax.random.fold_in(splits[16], 71), 0)
    node_cot = draw_node_cot(jax.random.fold_in(splits[16], 71), 0)
    edge_length = jnp.clip(0.5 + 5.0 * jax.random.uniform(splits[2], (SYSTEMS, EDGE_SLOTS), jnp.float32) ** level_of(splits[2], (SYSTEMS, EDGE_SLOTS), ((0, 512),), -0.2, 0.2), 0.5, 5.5)
    atom_count = draw_atom_count(jax.random.fold_in(splits[16], 71), 0)
    edge_count = draw_edge_count(jax.random.fold_in(splits[16], 71), 0)
    edge_source = draw_edge_source(jax.random.fold_in(splits[16], 71), 0)
    edge_target = draw_edge_target(jax.random.fold_in(splits[16], 71), 0)
    dataset_tag = touch_ends(jax.random.randint(splits[7], (SYSTEMS,), 0, DATASETS), jax.random.fold_in(splits[7], 1), 0, DATASETS - 1).astype(jnp.int32)
    charge_tag = touch_ends(jax.random.randint(splits[8], (SYSTEMS,), 0, CHARGES), jax.random.fold_in(splits[8], 1), 0, CHARGES - 1).astype(jnp.int32)
    spin_tag = touch_ends(jax.random.randint(splits[9], (SYSTEMS,), 0, SPINS), jax.random.fold_in(splits[9], 1), 0, SPINS - 1).astype(jnp.int32)
    dataset_gain = jnp.clip(jnp.exp(jax.random.uniform(splits[10], (DATASETS, EXPERTS), jnp.float32, math.log(0.2), math.log(5.0))), 0.2, 5.0)
    charge_gain = jnp.clip(jnp.exp(jax.random.uniform(splits[11], (CHARGES, EXPERTS), jnp.float32, math.log(0.2), math.log(5.0))), 0.2, 5.0)
    spin_gain = jnp.clip(jnp.exp(jax.random.uniform(splits[12], (SPINS, EXPERTS), jnp.float32, math.log(0.2), math.log(5.0))), 0.2, 5.0)
    params = centred(splits[13], (EXPERTS, CH, 2, CH), (2 * CH) ** -0.5, 0.375, ((1, 32),), jnp.float32)
    moment_one = centred(splits[14], (EXPERTS, CH, 2, CH), 0.15, 0.9, ((1, 32),), jnp.float32)
    moment_two = jnp.clip(jnp.exp(math.log(0.01) - 4.6051702 * jax.random.uniform(splits[15], (EXPERTS, CH, 2, CH), jnp.float32) ** level_of(splits[15], (EXPERTS, CH, 2, CH), ((1, 32),), -0.2, 0.2)), 0.0001, 0.01)
    return {"node_feat": node_feat, "node_cot": node_cot, "edge_length": edge_length, "atom_count": atom_count, "edge_count": edge_count, "edge_source": edge_source, "edge_target": edge_target, "dataset_tag": dataset_tag, "charge_tag": charge_tag, "spin_tag": spin_tag, "dataset_gain": dataset_gain, "charge_gain": charge_gain, "spin_gain": spin_gain, "params": params, "moment_one": moment_one, "moment_two": moment_two}


beta_one = 0.9
beta_two = 0.999
adam_eps = 1e-08
learn_rate = 0.01
decay_rate = 0.01
cutoff_radius = 6.0

def envelope(length):
    ratio = length / cutoff_radius
    return 1.0 - 21.0 * ratio ** 5 + 35.0 * ratio ** 6 - 15.0 * ratio ** 7

def pick_rows(node_rows, slot_ids):
    return node_rows[slot_ids]

def mixing_table(dataset_gain, charge_gain, spin_gain):
    product_table = dataset_gain[:, None, None, :] * charge_gain[None, :, None, :] * spin_gain[None, None, :, :]
    product_table = product_table.reshape(-1, product_table.shape[-1])
    return product_table / lax.optimization_barrier(jnp.sum(product_table, axis=1, keepdims=True))

def onehot_rows(dataset_tag, charge_tag, spin_tag, charge_count, spin_count, row_total):
    tag_rows = (dataset_tag * charge_count + charge_tag) * spin_count + spin_tag
    return (tag_rows[:, None] == jnp.arange(row_total, dtype=jnp.int32)[None, :]).astype(jnp.float32)

def edge_cotangent(node_cot, edge_target, edge_count, atom_count, atom_slots):
    picked = jax.vmap(pick_rows)(node_cot, edge_target)
    slot_index = lax.broadcasted_iota(jnp.int32, edge_target.shape, 1)
    live_mask = (slot_index < edge_count[:, None]).astype(jnp.float32)
    atom_weight = float(atom_slots) / atom_count.astype(jnp.float32)
    factor = live_mask * atom_weight[:, None]
    return (picked.astype(jnp.float32) * factor[:, :, None]).astype(jnp.bfloat16)

def adam_update(gradients, params, moment_one, moment_two, square_sum, norm_limit):
    clip_factor = jnp.minimum(1.0, norm_limit / (jnp.sqrt(square_sum) + 1e-06))
    clipped = clip_factor * gradients
    new_one = beta_one * moment_one + (1.0 - beta_one) * clipped
    new_two = beta_two * moment_two + (1.0 - beta_two) * clipped * clipped
    first_fix = 1.0 - beta_one ** STEP
    second_fix = 1.0 - beta_two ** STEP
    direction = new_one / first_fix / (jnp.sqrt(new_two / second_fix) + adam_eps)
    new_params = params - learn_rate * (direction + decay_rate * params)
    return (new_params, new_one, new_two)

def reference(node_feat, node_cot, edge_length, atom_count, edge_count, edge_source, edge_target, dataset_tag, charge_tag, spin_tag, dataset_gain, charge_gain, spin_gain, params, moment_one, moment_two):
    mixing = mixing_table(dataset_gain, charge_gain, spin_gain)
    row_total = DATASETS * CHARGES * SPINS
    tag_onehot = onehot_rows(dataset_tag, charge_tag, spin_tag, CHARGES, SPINS, row_total)
    block_count = SYSTEMS // SYS_DEV

    def by_block(array):
        return array.reshape((block_count, SYS_DEV) + array.shape[1:])

    def scan_step(running, block_items):
        feat_block, cot_block, length_block, atoms_block, edges_block, source_block, target_block, onehot_block = block_items
        edge_grad = edge_cotangent(cot_block, target_block, edges_block, atoms_block, ATOMS)
        picked = jax.vmap(pick_rows)(feat_block, source_block)
        edge_input = (picked.astype(jnp.float32) * envelope(length_block)[:, :, None]).astype(jnp.bfloat16)
        products = jnp.einsum('sja,sjb->sab', edge_input.astype(jnp.float32), edge_grad.astype(jnp.float32), precision=lax.Precision.HIGHEST)
        real_part = products[:, :CH, :CH] + products[:, CH:, CH:]
        imag_part = products[:, :CH, CH:] - products[:, CH:, :CH]
        system_grad = jnp.stack([real_part, imag_part], axis=2)
        added = jnp.einsum('sk,scto->ckto', onehot_block, system_grad, precision=lax.Precision.HIGHEST)
        return (running + added, None)
    initial = jnp.zeros((CH, row_total, 2, CH), jnp.float32)
    blocks = tuple((by_block(array) for array in (node_feat, node_cot, edge_length, atom_count, edge_count, edge_source, edge_target, tag_onehot)))
    grouped, _ = lax.scan(scan_step, initial, blocks)
    gradients = jnp.einsum('ke,ckto->ecto', mixing, grouped, precision=lax.Precision.HIGHEST)
    square_sum = jnp.sum(gradients * gradients)
    norm_limit = math.sqrt(EXPERTS * 2 * CH * CH)
    new_params, new_one, new_two = adam_update(gradients, params, moment_one, moment_two, square_sum, norm_limit)
    return (new_params, new_one, new_two, new_params.astype(jnp.bfloat16))
```

```python
import functools
import math

import jax
import jax.numpy as jnp
from jax import lax
from jax.experimental import pallas as pl
from jax.experimental.pallas import tpu as pltpu
from jax.sharding import PartitionSpec as P

STEP = 10

beta_one = 0.9
beta_two = 0.999
adam_eps = 1e-08
learn_rate = 0.01
decay_rate = 0.01
cutoff_radius = 6.0

EDGE_BLOCK = 512


def envelope(length):
    ratio = length / cutoff_radius
    return 1.0 - 21.0 * ratio**5 + 35.0 * ratio**6 - 15.0 * ratio**7


def grouped_kernel(
    data_tag,
    charge_tag,
    spin_tag,
    atoms_ref,
    edges_ref,
    feat_ref,
    cot_ref,
    length_ref,
    source_ref,
    target_ref,
    out_ref,
    total,
    product,
):
    system = pl.program_id(0)
    atom_slots, width = feat_ref.shape[1:]
    channels = width // 2
    slots = length_ref.shape[1]

    @pl.when(system == 0)
    def _():
        total[...] = jnp.zeros_like(total)

    feat = feat_ref[0].T
    cot = cot_ref[0].T
    edges_here = edges_ref[system]
    weight = jnp.full((1, EDGE_BLOCK), float(atom_slots), jnp.float32) / jnp.full(
        (1, EDGE_BLOCK), atoms_ref[system], jnp.int32
    ).astype(jnp.float32)
    atom_ids = lax.broadcasted_iota(jnp.int32, (atom_slots, EDGE_BLOCK), 0)
    slot_ids = lax.broadcasted_iota(jnp.int32, (1, EDGE_BLOCK), 1)
    row = pl.ds(system, 1)

    for block in range(slots // EDGE_BLOCK):
        first = block * EDGE_BLOCK

        def step(first=first, block=block):
            cols = pl.ds(first, EDGE_BLOCK)
            pick_source = (atom_ids == source_ref[row, cols]).astype(jnp.float32).astype(jnp.bfloat16)
            pick_target = (atom_ids == target_ref[row, cols]).astype(jnp.float32).astype(jnp.bfloat16)
            edge_input = jnp.dot(feat, pick_source, preferred_element_type=jnp.float32)
            edge_input = (edge_input * envelope(length_ref[row, cols])).astype(jnp.bfloat16)
            factor = jnp.where(slot_ids + first < edges_here, weight, 0.0)
            edge_grad = jnp.dot(cot, pick_target, preferred_element_type=jnp.float32)
            edge_grad = (edge_grad * factor).astype(jnp.bfloat16)
            part = lax.dot_general(
                edge_input,
                edge_grad,
                (((1,), (1,)), ((), ())),
                preferred_element_type=jnp.float32,
            )
            if block == 0:
                product[...] = part
            else:
                product[...] += part

        if block == 0:
            step()
        else:
            pl.when(first < edges_here)(step)

    tag = (data_tag[system] * 2 + charge_tag[system]) * 2 + spin_tag[system]
    total[2 * tag] += product[:channels, :channels] + product[channels:, channels:]
    total[2 * tag + 1] += product[:channels, channels:] - product[channels:, :channels]

    @pl.when(system == pl.num_programs(0) - 1)
    def _():
        out_ref[...] = total[...].astype(out_ref.dtype)


def grouped_sums(feat, cot, length, atoms, edges, source, target, data_tag, charge_tag, spin_tag):
    systems, atom_slots, width = feat.shape
    channels = width // 2
    slots = length.shape[1]
    whole = lambda i, *_: (0, 0)
    each = lambda i, *_: (i, 0, 0)
    return pl.pallas_call(
        grouped_kernel,
        out_shape=jax.ShapeDtypeStruct((16, channels, channels), jnp.bfloat16),
        grid_spec=pltpu.PrefetchScalarGridSpec(
            num_scalar_prefetch=5,
            grid=(systems,),
            in_specs=[
                pl.BlockSpec((1, atom_slots, width), each),
                pl.BlockSpec((1, atom_slots, width), each),
                pl.BlockSpec((systems, slots), whole),
                pl.BlockSpec((systems, slots), whole),
                pl.BlockSpec((systems, slots), whole),
            ],
            out_specs=pl.BlockSpec((16, channels, channels), lambda i, *_: (0, 0, 0)),
            scratch_shapes=[
                pltpu.VMEM((16, channels, channels), jnp.float32),
                pltpu.VMEM((width, width), jnp.float32),
            ],
        ),
        name="grouped_sums",
    )(data_tag, charge_tag, spin_tag, atoms, edges, feat, cot, length, source, target)


def expert_kernel(data_ref, charge_ref, spin_ref, sums_ref, grad_ref, square_ref):
    data_gain, charge_gain, spin_gain = data_ref[...], charge_ref[...], spin_ref[...]
    table = jnp.concatenate(
        [
            data_gain[d : d + 1] * charge_gain[c : c + 1] * spin_gain[s : s + 1]
            for d in range(2)
            for c in range(2)
            for s in range(2)
        ],
        axis=0,
    )
    mixing = table / jnp.sum(table, axis=1, keepdims=True)
    squares = None
    for channel in range(4):
        for part in range(2):
            rows = sums_ref[:, part, channel, :]
            grad = lax.dot_general(
                mixing,
                rows,
                (((0,), (0,)), ((), ())),
                precision=lax.Precision.HIGHEST,
                preferred_element_type=jnp.float32,
            )
            grad_ref[:, 2 * channel + part, :] = grad
            term = jnp.sum(grad * grad, axis=0, keepdims=True)
            squares = term if squares is None else squares + term
    square_ref[...] = jnp.broadcast_to(squares[None], square_ref.shape)


def expert_grads(data_gain, charge_gain, spin_gain, sums, shards):
    experts = data_gain.shape[1]
    return pl.pallas_call(
        expert_kernel,
        out_shape=(
            jax.ShapeDtypeStruct((experts, 8, 128), jnp.float32),
            jax.ShapeDtypeStruct((shards, 1, 128), jnp.float32),
        ),
        name="expert_grads",
    )(data_gain, charge_gain, spin_gain, sums)


def adam_kernel(
    norm_limit,
    first_ref,
    square_ref,
    grad_ref,
    params_ref,
    one_ref,
    two_ref,
    new_params_ref,
    new_one_ref,
    new_two_ref,
    share_ref,
):
    squares = jnp.sum(square_ref[...], axis=0)
    square_sum = jnp.sum(squares, axis=1, keepdims=True)
    clip_factor = jnp.minimum(1.0, norm_limit / (jnp.sqrt(square_sum) + 1e-06))
    clipped = clip_factor[None] * grad_ref[...]
    new_one = beta_one * one_ref[...] + (1.0 - beta_one) * clipped
    new_two = beta_two * two_ref[...] + (1.0 - beta_two) * clipped * clipped
    first_fix = 1.0 - beta_one**STEP
    second_fix = 1.0 - beta_two**STEP
    direction = new_one / first_fix / (jnp.sqrt(new_two / second_fix) + adam_eps)
    params = params_ref[...]
    new_params_ref[...] = params - learn_rate * (direction + decay_rate * params)
    new_one_ref[...] = new_one
    new_two_ref[...] = new_two
    mine = new_params_ref[pl.ds(first_ref[0], 2)].reshape(16, 128).astype(jnp.bfloat16)
    share_ref[...] = jnp.broadcast_to(mine[None], share_ref.shape)


def adam_update(first, squares, grads, params, moment_one, moment_two, norm_limit):
    shards = squares.shape[0]
    state = jax.ShapeDtypeStruct(params.shape, jnp.float32)
    vmem = pl.BlockSpec(memory_space=pltpu.VMEM)
    return pl.pallas_call(
        functools.partial(adam_kernel, norm_limit),
        out_shape=(state, state, state, jax.ShapeDtypeStruct((shards, 16, 128), jnp.bfloat16)),
        in_specs=[pl.BlockSpec(memory_space=pltpu.SMEM)] + [vmem] * 5,
        out_specs=(vmem,) * 4,
        name="adam_update",
    )(first, squares, grads, params, moment_one, moment_two)


def exchange(array, axis, groups=None):
    return lax.all_to_all(array, axis, 0, 0, axis_index_groups=groups, tiled=True)


def local(
    node_feat,
    node_cot,
    edge_length,
    atom_count,
    edge_count,
    edge_source,
    edge_target,
    dataset_tag,
    charge_tag,
    spin_tag,
    dataset_gain,
    charge_gain,
    spin_gain,
    params,
    moment_one,
    moment_two,
):
    channels = node_feat.shape[2] // 2
    shards, reps = 32, 16
    experts, own = params.shape[:2]
    shape = params.shape
    rows = (experts, own * 2, channels)
    place = lax.axis_index("rep")
    first = jnp.bitwise_and(place, 1) * (experts // 2) + jnp.bitwise_and(place, reps - 2)

    sums = grouped_sums(
        node_feat,
        node_cot,
        edge_length,
        atom_count,
        edge_count,
        edge_source,
        edge_target,
        dataset_tag,
        charge_tag,
        spin_tag,
    )
    sums = exchange(sums, "rep")
    sums = jnp.sum(sums.astype(jnp.float32), axis=0).reshape(shards, own, channels)
    sums = exchange(sums, "shard")
    sums = jnp.sum(sums, axis=0)
    sums = exchange(jnp.broadcast_to(sums[None], (reps, own, channels)), "rep")
    grads, squares = expert_grads(
        dataset_gain, charge_gain, spin_gain, sums.reshape(8, 2, own, channels), shards
    )
    squares = exchange(squares, "shard")
    norm_limit = math.sqrt(experts * 2 * channels * channels)
    new_params, new_one, new_two, share = adam_update(
        first.reshape(1),
        squares,
        grads,
        params.reshape(rows),
        moment_one.reshape(rows),
        moment_two.reshape(rows),
        norm_limit,
    )
    share = exchange(share, "shard").reshape(shards, 2, own * 2, channels)
    share = jnp.broadcast_to(jnp.swapaxes(share, 0, 1)[None], (8, 2, shards, own * 2, channels))
    share = exchange(share, "rep", [[2 * i + core for i in range(8)] for core in range(2)])
    share = jnp.broadcast_to(share[None], (2,) + share.shape)
    share = exchange(share, "rep", [[2 * i, 2 * i + 1] for i in range(8)])
    full_weights = share.reshape(experts, shards * own, 2, channels)
    return (new_params.reshape(shape), new_one.reshape(shape), new_two.reshape(shape), full_weights)


def solution(mesh):
    placed = (
        P(("shard", "rep"), None, None),
        P(("shard", "rep"), None, None),
        P(("shard", "rep"), None),
        P(("shard", "rep")),
        P(("shard", "rep")),
        P(("shard", "rep"), None),
        P(("shard", "rep"), None),
        P(("shard", "rep")),
        P(("shard", "rep")),
        P(("shard", "rep")),
        P(),
        P(),
        P(),
        P(None, "shard", None, None),
        P(None, "shard", None, None),
        P(None, "shard", None, None),
    )
    return jax.shard_map(
        local,
        mesh=mesh,
        in_specs=placed,
        out_specs=(
            P(None, "shard", None, None),
            P(None, "shard", None, None),
            P(None, "shard", None, None),
            P(),
        ),
        check_vma=False,
    )
```

```python
import functools
import math

import jax
import jax.numpy as jnp
from jax import lax
from jax.experimental import pallas as pl
from jax.experimental.pallas import tpu as pltpu
from jax.sharding import PartitionSpec as P

STEP = 10

beta_one = 0.9
beta_two = 0.999
adam_eps = 1e-08
learn_rate = 0.01
decay_rate = 0.01
cutoff_radius = 6.0

HELD = 4
PARAMS = pltpu.CompilerParams(vmem_limit_bytes=24 * 2**20)


def envelope(length):
    ratio = length / cutoff_radius
    return 1.0 - 21.0 * ratio**5 + 35.0 * ratio**6 - 15.0 * ratio**7


def grouped_kernel(
    data_tag,
    charge_tag,
    spin_tag,
    atoms_ref,
    edges_ref,
    feat_ref,
    cot_ref,
    length_ref,
    source_ref,
    target_ref,
    out_ref,
    total,
):
    step = pl.program_id(0)
    held, atom_slots, width = feat_ref.shape
    channels = width // 2
    slots = length_ref.shape[1]

    @pl.when(step == 0)
    def _():
        total[...] = jnp.zeros_like(total)

    atom_ids = lax.broadcasted_iota(jnp.int32, (atom_slots, slots), 0)
    atom_ids = atom_ids.astype(jnp.float32).astype(jnp.bfloat16)
    zero = jnp.zeros((atom_slots, slots), jnp.bfloat16)
    one = jnp.ones((atom_slots, slots), jnp.bfloat16)
    slot_ids = lax.broadcasted_iota(jnp.int32, (1, slots), 1)
    for index in range(held):
        system = step * held + index
        row = pl.ds(system, 1)
        atoms_here = jnp.full((1, slots), atoms_ref[system], jnp.int32).astype(jnp.float32)
        weight = envelope(length_ref[row, :]) * (float(atom_slots) / atoms_here)
        weight = jnp.where(slot_ids < edges_ref[system], weight, 0.0).astype(jnp.bfloat16)
        source = source_ref[row, :].astype(jnp.float32).astype(jnp.bfloat16)
        target = target_ref[row, :].astype(jnp.float32).astype(jnp.bfloat16)
        links = lax.dot_general(
            jnp.where(atom_ids == source, weight, zero),
            jnp.where(atom_ids == target, one, zero),
            (((1,), (1,)), ((), ())),
            preferred_element_type=jnp.float32,
        ).astype(jnp.bfloat16)
        mixed = jnp.dot(links, cot_ref[index], preferred_element_type=jnp.float32)
        product = jnp.dot(
            feat_ref[index].T, mixed.astype(jnp.bfloat16), preferred_element_type=jnp.float32
        )
        tag = (data_tag[system] * 2 + charge_tag[system]) * 2 + spin_tag[system]
        total[2 * tag] += product[:channels, :channels] + product[channels:, channels:]
        total[2 * tag + 1] += product[:channels, channels:] - product[channels:, :channels]

    @pl.when(step == pl.num_programs(0) - 1)
    def _():
        out_ref[...] = total[...].astype(out_ref.dtype)


def grouped_sums(feat, cot, length, atoms, edges, source, target, data_tag, charge_tag, spin_tag):
    systems, atom_slots, width = feat.shape
    channels = width // 2
    slots = length.shape[1]
    whole = lambda i, *_: (0, 0)
    each = lambda i, *_: (i, 0, 0)
    return pl.pallas_call(
        grouped_kernel,
        out_shape=jax.ShapeDtypeStruct((16, channels, channels), jnp.bfloat16),
        grid_spec=pltpu.PrefetchScalarGridSpec(
            num_scalar_prefetch=5,
            grid=(systems // HELD,),
            in_specs=[
                pl.BlockSpec((HELD, atom_slots, width), each),
                pl.BlockSpec((HELD, atom_slots, width), each),
                pl.BlockSpec((systems, slots), whole),
                pl.BlockSpec((systems, slots), whole),
                pl.BlockSpec((systems, slots), whole),
            ],
            out_specs=pl.BlockSpec((16, channels, channels), lambda i, *_: (0, 0, 0)),
            scratch_shapes=[pltpu.VMEM((16, channels, channels), jnp.float32)],
        ),
        name="grouped_sums",
    )(data_tag, charge_tag, spin_tag, atoms, edges, feat, cot, length, source, target)


def expert_kernel(data_ref, charge_ref, spin_ref, sums_ref, grad_ref, square_ref):
    data_gain, charge_gain, spin_gain = data_ref[...], charge_ref[...], spin_ref[...]
    table = jnp.concatenate(
        [
            data_gain[d : d + 1] * charge_gain[c : c + 1] * spin_gain[s : s + 1]
            for d in range(2)
            for c in range(2)
            for s in range(2)
        ],
        axis=0,
    )
    mixing = table / jnp.sum(table, axis=1, keepdims=True)
    squares = None
    for channel in range(4):
        for part in range(2):
            rows = sums_ref[:, part, channel, :]
            grad = lax.dot_general(
                mixing,
                rows,
                (((0,), (0,)), ((), ())),
                precision=lax.Precision.HIGHEST,
                preferred_element_type=jnp.float32,
            )
            grad_ref[:, 2 * channel + part, :] = grad
            term = jnp.sum(grad * grad, axis=0, keepdims=True)
            squares = term if squares is None else squares + term
    square_ref[...] = jnp.broadcast_to(squares[None], square_ref.shape)


def expert_grads(data_gain, charge_gain, spin_gain, sums, shards):
    experts = data_gain.shape[1]
    return pl.pallas_call(
        expert_kernel,
        out_shape=(
            jax.ShapeDtypeStruct((experts, 8, 128), jnp.float32),
            jax.ShapeDtypeStruct((shards, 1, 128), jnp.float32),
        ),
        compiler_params=PARAMS,
        name="expert_grads",
    )(data_gain, charge_gain, spin_gain, sums)


def adam_kernel(
    norm_limit,
    first_ref,
    square_ref,
    grad_ref,
    params_ref,
    one_ref,
    two_ref,
    new_params_ref,
    new_one_ref,
    new_two_ref,
    share_ref,
):
    squares = jnp.sum(square_ref[...], axis=0)
    square_sum = jnp.sum(squares, axis=1, keepdims=True)
    clip_factor = jnp.minimum(1.0, norm_limit / (jnp.sqrt(square_sum) + 1e-06))
    clipped = clip_factor[None] * grad_ref[...]
    new_one = beta_one * one_ref[...] + (1.0 - beta_one) * clipped
    new_two = beta_two * two_ref[...] + (1.0 - beta_two) * clipped * clipped
    first_fix = 1.0 - beta_one**STEP
    second_fix = 1.0 - beta_two**STEP
    direction = new_one / first_fix / (jnp.sqrt(new_two / second_fix) + adam_eps)
    params = params_ref[...]
    new_params_ref[...] = params - learn_rate * (direction + decay_rate * params)
    new_one_ref[...] = new_one
    new_two_ref[...] = new_two
    mine = new_params_ref[pl.ds(first_ref[0], 2)].reshape(16, 128).astype(jnp.bfloat16)
    share_ref[...] = jnp.broadcast_to(mine[None], share_ref.shape)


def adam_update(first, squares, grads, params, moment_one, moment_two, norm_limit):
    shards = squares.shape[0]
    state = jax.ShapeDtypeStruct(params.shape, jnp.float32)
    vmem = pl.BlockSpec(memory_space=pltpu.VMEM)
    return pl.pallas_call(
        functools.partial(adam_kernel, norm_limit),
        out_shape=(state, state, state, jax.ShapeDtypeStruct((shards, 16, 128), jnp.bfloat16)),
        in_specs=[pl.BlockSpec(memory_space=pltpu.SMEM)] + [vmem] * 5,
        out_specs=(vmem,) * 4,
        compiler_params=PARAMS,
        name="adam_update",
    )(first, squares, grads, params, moment_one, moment_two)


def exchange(array, axis, groups=None):
    return lax.all_to_all(array, axis, 0, 0, axis_index_groups=groups, tiled=True)


def local(
    node_feat,
    node_cot,
    edge_length,
    atom_count,
    edge_count,
    edge_source,
    edge_target,
    dataset_tag,
    charge_tag,
    spin_tag,
    dataset_gain,
    charge_gain,
    spin_gain,
    params,
    moment_one,
    moment_two,
):
    channels = node_feat.shape[2] // 2
    shards, reps = 32, 16
    experts, own = params.shape[:2]
    shape = params.shape
    rows = (experts, own * 2, channels)
    place = lax.axis_index("rep")
    first = jnp.bitwise_and(place, 1) * (experts // 2) + jnp.bitwise_and(place, reps - 2)

    sums = grouped_sums(
        node_feat,
        node_cot,
        edge_length,
        atom_count,
        edge_count,
        edge_source,
        edge_target,
        dataset_tag,
        charge_tag,
        spin_tag,
    )
    sums = exchange(sums, "rep")
    sums = jnp.sum(sums.astype(jnp.float32), axis=0).reshape(shards, own, channels)
    sums = exchange(sums, "shard")
    sums = jnp.sum(sums, axis=0)
    sums = exchange(jnp.broadcast_to(sums[None], (reps, own, channels)), "rep")
    grads, squares = expert_grads(
        dataset_gain, charge_gain, spin_gain, sums.reshape(8, 2, own, channels), shards
    )
    squares = exchange(squares, "shard")
    norm_limit = math.sqrt(experts * 2 * channels * channels)
    new_params, new_one, new_two, share = adam_update(
        first.reshape(1),
        squares,
        grads,
        params.reshape(rows),
        moment_one.reshape(rows),
        moment_two.reshape(rows),
        norm_limit,
    )
    share = exchange(share, "shard").reshape(shards, 2, own * 2, channels)
    share = jnp.broadcast_to(jnp.swapaxes(share, 0, 1)[None], (8, 2, shards, own * 2, channels))
    share = exchange(share, "rep", [[2 * i + core for i in range(8)] for core in range(2)])
    share = jnp.broadcast_to(share[None], (2,) + share.shape)
    share = exchange(share, "rep", [[2 * i, 2 * i + 1] for i in range(8)])
    full_weights = share.reshape(experts, shards * own, 2, channels)
    return (new_params.reshape(shape), new_one.reshape(shape), new_two.reshape(shape), full_weights)


def solution(mesh):
    placed = (
        P(("shard", "rep"), None, None),
        P(("shard", "rep"), None, None),
        P(("shard", "rep"), None),
        P(("shard", "rep")),
        P(("shard", "rep")),
        P(("shard", "rep"), None),
        P(("shard", "rep"), None),
        P(("shard", "rep")),
        P(("shard", "rep")),
        P(("shard", "rep")),
        P(),
        P(),
        P(),
        P(None, "shard", None, None),
        P(None, "shard", None, None),
        P(None, "shard", None, None),
    )
    return jax.shard_map(
        local,
        mesh=mesh,
        in_specs=placed,
        out_specs=(
            P(None, "shard", None, None),
            P(None, "shard", None, None),
            P(None, "shard", None, None),
            P(),
        ),
        check_vma=False,
    )
```

```python
import functools
import math

import jax
import jax.numpy as jnp
from jax import lax
from jax.experimental import pallas as pl
from jax.experimental.pallas import tpu as pltpu
from jax.sharding import PartitionSpec as P

STEP = 10

beta_one = 0.9
beta_two = 0.999
adam_eps = 1e-08
learn_rate = 0.01
decay_rate = 0.01
cutoff_radius = 6.0

PARAMS = pltpu.CompilerParams(vmem_limit_bytes=24 * 2**20)


def envelope(length):
    ratio = length / cutoff_radius
    return 1.0 - 21.0 * ratio**5 + 35.0 * ratio**6 - 15.0 * ratio**7


def grouped_kernel(
    data_tag,
    charge_tag,
    spin_tag,
    atoms_ref,
    edges_ref,
    feat_ref,
    cot_ref,
    length_ref,
    source_ref,
    target_ref,
    out_ref,
    total,
):
    systems, atom_slots, width = feat_ref.shape
    channels = width // 2
    slots = length_ref.shape[1]
    total[...] = jnp.zeros_like(total)

    atom_ids = lax.broadcasted_iota(jnp.int32, (atom_slots, slots), 0)
    atom_ids = atom_ids.astype(jnp.float32).astype(jnp.bfloat16)
    zero = jnp.zeros((atom_slots, slots), jnp.bfloat16)
    one = jnp.ones((atom_slots, slots), jnp.bfloat16)
    system_ids = lax.broadcasted_iota(jnp.int32, (systems, slots), 0)
    slot_ids = lax.broadcasted_iota(jnp.int32, (systems, slots), 1)
    atoms = jnp.zeros((systems, slots), jnp.int32)
    edges = jnp.zeros((systems, slots), jnp.int32)
    for system in range(systems):
        atoms = jnp.where(system_ids == system, atoms_ref[system], atoms)
        edges = jnp.where(system_ids == system, edges_ref[system], edges)
    weight = envelope(length_ref[...]) * (float(atom_slots) / atoms.astype(jnp.float32))
    weight = jnp.where(slot_ids < edges, weight, 0.0).astype(jnp.bfloat16)
    source = source_ref[...].astype(jnp.float32).astype(jnp.bfloat16)
    target = target_ref[...].astype(jnp.float32).astype(jnp.bfloat16)

    links = []
    for system in range(systems):
        row = slice(system, system + 1)
        links.append(
            lax.dot_general(
                jnp.where(atom_ids == source[row], weight[row], zero),
                jnp.where(atom_ids == target[row], one, zero),
                (((1,), (1,)), ((), ())),
                preferred_element_type=jnp.float32,
            ).astype(jnp.bfloat16)
        )
    for system in range(systems):
        mixed = jnp.dot(links[system], cot_ref[system], preferred_element_type=jnp.float32)
        mixed = mixed.astype(jnp.bfloat16)
        swapped = jnp.concatenate([mixed[:, channels:], -mixed[:, :channels]], axis=1)
        feat = feat_ref[system]
        product = jnp.dot(
            jnp.concatenate([feat[:, :channels].T, feat[:, channels:].T], axis=1),
            jnp.concatenate([mixed, swapped], axis=0),
            preferred_element_type=jnp.float32,
        )
        tag = (data_tag[system] * 2 + charge_tag[system]) * 2 + spin_tag[system]
        total[2 * tag] += product[:, :channels]
        total[2 * tag + 1] += product[:, channels:]
    out_ref[...] = total[...].astype(out_ref.dtype)


def grouped_sums(feat, cot, length, atoms, edges, source, target, data_tag, charge_tag, spin_tag):
    channels = feat.shape[2] // 2
    block = lambda shape: pl.BlockSpec(shape, lambda i: (0,) * len(shape))
    return pl.pallas_call(
        grouped_kernel,
        out_shape=jax.ShapeDtypeStruct((16, channels, channels), jnp.bfloat16),
        grid=(1,),
        in_specs=[pl.BlockSpec(memory_space=pltpu.SMEM)] * 5
        + [block(array.shape) for array in (feat, cot, length, source, target)],
        out_specs=block((16, channels, channels)),
        scratch_shapes=[pltpu.VMEM((16, channels, channels), jnp.float32)],
        name="grouped_sums",
    )(data_tag, charge_tag, spin_tag, atoms, edges, feat, cot, length, source, target)


def expert_kernel(data_ref, charge_ref, spin_ref, sums_ref, grad_ref, square_ref):
    data_gain, charge_gain, spin_gain = data_ref[...], charge_ref[...], spin_ref[...]
    table = jnp.concatenate(
        [
            data_gain[d : d + 1] * charge_gain[c : c + 1] * spin_gain[s : s + 1]
            for d in range(2)
            for c in range(2)
            for s in range(2)
        ],
        axis=0,
    )
    mixing = table / jnp.sum(table, axis=1, keepdims=True)
    squares = None
    for channel in range(4):
        for part in range(2):
            rows = sums_ref[:, part, channel, :]
            grad = lax.dot_general(
                mixing,
                rows,
                (((0,), (0,)), ((), ())),
                precision=lax.Precision.HIGHEST,
                preferred_element_type=jnp.float32,
            )
            grad_ref[:, 2 * channel + part, :] = grad
            term = jnp.sum(grad * grad, axis=0, keepdims=True)
            squares = term if squares is None else squares + term
    square_ref[...] = jnp.broadcast_to(squares[None], square_ref.shape)


def expert_grads(data_gain, charge_gain, spin_gain, sums, shards):
    experts = data_gain.shape[1]
    return pl.pallas_call(
        expert_kernel,
        out_shape=(
            jax.ShapeDtypeStruct((experts, 8, 128), jnp.float32),
            jax.ShapeDtypeStruct((shards, 1, 128), jnp.float32),
        ),
        compiler_params=PARAMS,
        name="expert_grads",
    )(data_gain, charge_gain, spin_gain, sums)


def adam_kernel(
    norm_limit,
    first_ref,
    square_ref,
    grad_ref,
    params_ref,
    one_ref,
    two_ref,
    new_params_ref,
    new_one_ref,
    new_two_ref,
    share_ref,
):
    squares = jnp.sum(square_ref[...], axis=0)
    square_sum = jnp.sum(squares, axis=1, keepdims=True)
    clip_factor = jnp.minimum(1.0, norm_limit / (jnp.sqrt(square_sum) + 1e-06))
    clipped = clip_factor[None] * grad_ref[...]
    new_one = beta_one * one_ref[...] + (1.0 - beta_one) * clipped
    new_two = beta_two * two_ref[...] + (1.0 - beta_two) * clipped * clipped
    first_fix = 1.0 - beta_one**STEP
    second_fix = 1.0 - beta_two**STEP
    direction = new_one / first_fix / (jnp.sqrt(new_two / second_fix) + adam_eps)
    params = params_ref[...]
    new_params_ref[...] = params - learn_rate * (direction + decay_rate * params)
    new_one_ref[...] = new_one
    new_two_ref[...] = new_two
    mine = new_params_ref[pl.ds(first_ref[0], 2)].reshape(16, 128).astype(jnp.bfloat16)
    share_ref[...] = jnp.broadcast_to(mine[None], share_ref.shape)


def adam_update(first, squares, grads, params, moment_one, moment_two, norm_limit):
    shards = squares.shape[0]
    state = jax.ShapeDtypeStruct(params.shape, jnp.float32)
    vmem = pl.BlockSpec(memory_space=pltpu.VMEM)
    return pl.pallas_call(
        functools.partial(adam_kernel, norm_limit),
        out_shape=(state, state, state, jax.ShapeDtypeStruct((shards, 16, 128), jnp.bfloat16)),
        in_specs=[pl.BlockSpec(memory_space=pltpu.SMEM)] + [vmem] * 5,
        out_specs=(vmem,) * 4,
        compiler_params=PARAMS,
        name="adam_update",
    )(first, squares, grads, params, moment_one, moment_two)


def place_kernel(offset, core_ref, *refs):
    half_ref, out_ref, sem = refs[0], refs[-2], refs[-1]
    side = jnp.bitwise_xor(core_ref[0], offset)
    copy = pltpu.make_async_copy(half_ref, out_ref.at[side], sem)
    copy.start()
    copy.wait()


def place_half(offset, core, half, *held):
    hbm = pl.BlockSpec(memory_space=pl.ANY)
    return pl.pallas_call(
        functools.partial(place_kernel, offset),
        out_shape=jax.ShapeDtypeStruct((2,) + half.shape, half.dtype),
        in_specs=[
            pl.BlockSpec(memory_space=pltpu.SMEM),
            pl.BlockSpec(memory_space=pltpu.VMEM),
        ]
        + [hbm] * len(held),
        out_specs=hbm,
        scratch_shapes=[pltpu.SemaphoreType.DMA],
        input_output_aliases={2: 0} if held else {},
        compiler_params=PARAMS,
        cost_estimate=pl.CostEstimate(
            flops=0, transcendentals=0, bytes_accessed=2 * half.size * half.dtype.itemsize
        ),
        name="place_half",
    )(core, half, *held)


def exchange(array, axis, groups=None):
    return lax.all_to_all(array, axis, 0, 0, axis_index_groups=groups, tiled=True)


def local(
    node_feat,
    node_cot,
    edge_length,
    atom_count,
    edge_count,
    edge_source,
    edge_target,
    dataset_tag,
    charge_tag,
    spin_tag,
    dataset_gain,
    charge_gain,
    spin_gain,
    params,
    moment_one,
    moment_two,
):
    channels = node_feat.shape[2] // 2
    shards, reps = 32, 16
    experts, own = params.shape[:2]
    shape = params.shape
    rows = (experts, own * 2, channels)
    place = lax.axis_index("rep")
    first = jnp.bitwise_and(place, 1) * (experts // 2) + jnp.bitwise_and(place, reps - 2)

    sums = grouped_sums(
        node_feat,
        node_cot,
        edge_length,
        atom_count,
        edge_count,
        edge_source,
        edge_target,
        dataset_tag,
        charge_tag,
        spin_tag,
    )
    sums = exchange(sums, "rep")
    sums = jnp.sum(sums.astype(jnp.float32), axis=0).reshape(shards, own, channels)
    sums = exchange(sums, "shard")
    sums = jnp.sum(sums, axis=0)
    sums = exchange(jnp.broadcast_to(sums[None], (reps, own, channels)), "rep")
    grads, squares = expert_grads(
        dataset_gain, charge_gain, spin_gain, sums.reshape(8, 2, own, channels), shards
    )
    squares = exchange(squares, "shard")
    norm_limit = math.sqrt(experts * 2 * channels * channels)
    new_params, new_one, new_two, share = adam_update(
        first.reshape(1),
        squares,
        grads,
        params.reshape(rows),
        moment_one.reshape(rows),
        moment_two.reshape(rows),
        norm_limit,
    )
    share = exchange(share, "shard").reshape(shards, 2, own * 2, channels)
    share = jnp.broadcast_to(jnp.swapaxes(share, 0, 1)[None], (8, 2, shards, own * 2, channels))
    share = exchange(share, "rep", [[2 * i + core for i in range(8)] for core in range(2)])
    core = jnp.bitwise_and(place, 1).reshape(1)
    other = lax.ppermute(share, "rep", [(i, i ^ 1) for i in range(reps)])
    full_weights = place_half(1, core, other, place_half(0, core, share))
    full_weights = full_weights.reshape(experts, shards * own, 2, channels)
    return (new_params.reshape(shape), new_one.reshape(shape), new_two.reshape(shape), full_weights)


def solution(mesh):
    placed = (
        P(("shard", "rep"), None, None),
        P(("shard", "rep"), None, None),
        P(("shard", "rep"), None),
        P(("shard", "rep")),
        P(("shard", "rep")),
        P(("shard", "rep"), None),
        P(("shard", "rep"), None),
        P(("shard", "rep")),
        P(("shard", "rep")),
        P(("shard", "rep")),
        P(),
        P(),
        P(),
        P(None, "shard", None, None),
        P(None, "shard", None, None),
        P(None, "shard", None, None),
    )
    return jax.shard_map(
        local,
        mesh=mesh,
        in_specs=placed,
        out_specs=(
            P(None, "shard", None, None),
            P(None, "shard", None, None),
            P(None, "shard", None, None),
            P(),
        ),
        check_vma=False,
    )
```

```python
import functools
import math

import jax
import jax.numpy as jnp
from jax import lax
from jax.experimental import pallas as pl
from jax.experimental.pallas import tpu as pltpu
from jax.sharding import PartitionSpec as P

STEP = 10

beta_one = 0.9
beta_two = 0.999
adam_eps = 1e-08
learn_rate = 0.01
decay_rate = 0.01
cutoff_radius = 6.0

PARAMS = pltpu.CompilerParams(vmem_limit_bytes=24 * 2**20)


def envelope(length):
    ratio = length / cutoff_radius
    return 1.0 - 21.0 * ratio**5 + 35.0 * ratio**6 - 15.0 * ratio**7


def grouped_kernel(
    data_tag,
    charge_tag,
    spin_tag,
    atoms_ref,
    edges_ref,
    feat_ref,
    cot_ref,
    length_ref,
    source_ref,
    target_ref,
    out_ref,
    total,
):
    systems, atom_slots, width = feat_ref.shape
    channels = width // 2
    slots = length_ref.shape[1]
    total[...] = jnp.zeros_like(total)

    atom_ids = lax.broadcasted_iota(jnp.int32, (atom_slots, slots), 0)
    atom_ids = atom_ids.astype(jnp.float32).astype(jnp.bfloat16)
    zero = jnp.zeros((atom_slots, slots), jnp.bfloat16)
    one = jnp.ones((atom_slots, slots), jnp.bfloat16)
    system_ids = lax.broadcasted_iota(jnp.int32, (systems, slots), 0)
    slot_ids = lax.broadcasted_iota(jnp.int32, (systems, slots), 1)
    atoms = jnp.zeros((systems, slots), jnp.int32)
    edges = jnp.zeros((systems, slots), jnp.int32)
    for system in range(systems):
        atoms = jnp.where(system_ids == system, atoms_ref[system], atoms)
        edges = jnp.where(system_ids == system, edges_ref[system], edges)
    weight = envelope(length_ref[...]) * (float(atom_slots) / atoms.astype(jnp.float32))
    weight = jnp.where(slot_ids < edges, weight, 0.0).astype(jnp.bfloat16)
    source = source_ref[...].astype(jnp.float32).astype(jnp.bfloat16)
    target = target_ref[...].astype(jnp.float32).astype(jnp.bfloat16)

    links = []
    for system in range(systems):
        row = slice(system, system + 1)
        links.append(
            lax.dot_general(
                jnp.where(atom_ids == source[row], weight[row], zero),
                jnp.where(atom_ids == target[row], one, zero),
                (((1,), (1,)), ((), ())),
                preferred_element_type=jnp.float32,
            ).astype(jnp.bfloat16)
        )
    for system in range(systems):
        mixed = jnp.dot(links[system], cot_ref[system], preferred_element_type=jnp.float32)
        mixed = mixed.astype(jnp.bfloat16)
        swapped = jnp.concatenate([mixed[:, channels:], -mixed[:, :channels]], axis=1)
        feat = feat_ref[system]
        product = jnp.dot(
            jnp.concatenate([feat[:, :channels].T, feat[:, channels:].T], axis=1),
            jnp.concatenate([mixed, swapped], axis=0),
            preferred_element_type=jnp.float32,
        )
        tag = (data_tag[system] * 2 + charge_tag[system]) * 2 + spin_tag[system]
        total[2 * tag] += product[:, :channels]
        total[2 * tag + 1] += product[:, channels:]
    half = channels // 2
    for side in range(2):
        rows = pl.ds(side * half, half)
        out_ref[pl.ds(16 * side, 16)] = total[:, rows, :].astype(out_ref.dtype)


def grouped_sums(feat, cot, length, atoms, edges, source, target, data_tag, charge_tag, spin_tag):
    channels = feat.shape[2] // 2
    block = lambda shape: pl.BlockSpec(shape, lambda i: (0,) * len(shape))
    return pl.pallas_call(
        grouped_kernel,
        out_shape=jax.ShapeDtypeStruct((32, channels // 2, channels), jnp.bfloat16),
        grid=(1,),
        in_specs=[pl.BlockSpec(memory_space=pltpu.SMEM)] * 5
        + [block(array.shape) for array in (feat, cot, length, source, target)],
        out_specs=block((32, channels // 2, channels)),
        scratch_shapes=[pltpu.VMEM((16, channels, channels), jnp.float32)],
        name="grouped_sums",
    )(data_tag, charge_tag, spin_tag, atoms, edges, feat, cot, length, source, target)


def expert_kernel(data_ref, charge_ref, spin_ref, sums_ref, grad_ref, square_ref):
    data_gain, charge_gain, spin_gain = data_ref[...], charge_ref[...], spin_ref[...]
    table = jnp.concatenate(
        [
            data_gain[d : d + 1] * charge_gain[c : c + 1] * spin_gain[s : s + 1]
            for d in range(2)
            for c in range(2)
            for s in range(2)
        ],
        axis=0,
    )
    mixing = table / jnp.sum(table, axis=1, keepdims=True)
    squares = None
    for channel in range(4):
        for part in range(2):
            rows = sums_ref[:, part, channel, :]
            grad = lax.dot_general(
                mixing,
                rows,
                (((0,), (0,)), ((), ())),
                precision=lax.Precision.HIGHEST,
                preferred_element_type=jnp.float32,
            )
            grad_ref[:, 2 * channel + part, :] = grad
            term = jnp.sum(grad * grad, axis=0, keepdims=True)
            squares = term if squares is None else squares + term
    square_ref[...] = jnp.broadcast_to(squares[None], square_ref.shape)


def expert_grads(data_gain, charge_gain, spin_gain, sums, shards):
    experts = data_gain.shape[1]
    return pl.pallas_call(
        expert_kernel,
        out_shape=(
            jax.ShapeDtypeStruct((experts, 8, 128), jnp.float32),
            jax.ShapeDtypeStruct((shards, 1, 128), jnp.float32),
        ),
        compiler_params=PARAMS,
        name="expert_grads",
    )(data_gain, charge_gain, spin_gain, sums)


def adam_kernel(
    norm_limit,
    first_ref,
    square_ref,
    grad_ref,
    params_ref,
    one_ref,
    two_ref,
    new_params_ref,
    new_one_ref,
    new_two_ref,
    share_ref,
):
    squares = jnp.sum(square_ref[...], axis=0)
    square_sum = jnp.sum(squares, axis=1, keepdims=True)
    clip_factor = jnp.minimum(1.0, norm_limit / (jnp.sqrt(square_sum) + 1e-06))
    clipped = clip_factor[None] * grad_ref[...]
    new_one = beta_one * one_ref[...] + (1.0 - beta_one) * clipped
    new_two = beta_two * two_ref[...] + (1.0 - beta_two) * clipped * clipped
    first_fix = 1.0 - beta_one**STEP
    second_fix = 1.0 - beta_two**STEP
    direction = new_one / first_fix / (jnp.sqrt(new_two / second_fix) + adam_eps)
    params = params_ref[...]
    new_params_ref[...] = params - learn_rate * (direction + decay_rate * params)
    new_one_ref[...] = new_one
    new_two_ref[...] = new_two
    mine = new_params_ref[pl.ds(first_ref[0], 2)].reshape(16, 128).astype(jnp.bfloat16)
    share_ref[...] = jnp.broadcast_to(mine[None], share_ref.shape)


def adam_update(first, squares, grads, params, moment_one, moment_two, norm_limit):
    state = jax.ShapeDtypeStruct(params.shape, jnp.float32)
    vmem = pl.BlockSpec(memory_space=pltpu.VMEM)
    return pl.pallas_call(
        functools.partial(adam_kernel, norm_limit),
        out_shape=(state, state, state, jax.ShapeDtypeStruct((16, 16, 128), jnp.bfloat16)),
        in_specs=[pl.BlockSpec(memory_space=pltpu.SMEM)] + [vmem] * 5,
        out_specs=(vmem,) * 4,
        compiler_params=PARAMS,
        name="adam_update",
    )(first, squares, grads, params, moment_one, moment_two)


def place_kernel(offset, core_ref, *refs):
    half_ref, out_ref, sems = refs[0], refs[-2], refs[-1]
    side = jnp.bitwise_xor(core_ref[0], offset)
    copies = [
        pltpu.make_async_copy(
            half_ref.at[:, low, expert], out_ref.at[side, :, expert, low], sems.at[2 * low + expert]
        )
        for low in range(2)
        for expert in range(2)
    ]
    for copy in copies:
        copy.start()
    for copy in copies:
        copy.wait()


def place_half(offset, core, half, *held):
    hbm = pl.BlockSpec(memory_space=pl.ANY)
    return pl.pallas_call(
        functools.partial(place_kernel, offset),
        out_shape=jax.ShapeDtypeStruct((2, 8, 2, 2) + half.shape[3:], half.dtype),
        in_specs=[
            pl.BlockSpec(memory_space=pltpu.SMEM),
            pl.BlockSpec(memory_space=pltpu.VMEM),
        ]
        + [hbm] * len(held),
        out_specs=hbm,
        scratch_shapes=[pltpu.SemaphoreType.DMA((4,))],
        input_output_aliases={2: 0} if held else {},
        compiler_params=PARAMS,
        cost_estimate=pl.CostEstimate(
            flops=0, transcendentals=0, bytes_accessed=2 * half.size * half.dtype.itemsize
        ),
        name="place_half",
    )(core, half, *held)


def exchange(array, axis, groups=None):
    return lax.all_to_all(array, axis, 0, 0, axis_index_groups=groups, tiled=True)


def local(
    node_feat,
    node_cot,
    edge_length,
    atom_count,
    edge_count,
    edge_source,
    edge_target,
    dataset_tag,
    charge_tag,
    spin_tag,
    dataset_gain,
    charge_gain,
    spin_gain,
    params,
    moment_one,
    moment_two,
):
    channels = node_feat.shape[2] // 2
    shards, reps = 32, 16
    experts, own = params.shape[:2]
    shape = params.shape
    rows = (experts, own * 2, channels)
    place = lax.axis_index("rep")
    first = jnp.bitwise_and(place, 1) * (experts // 2) + jnp.bitwise_and(place, reps - 2)
    core = jnp.bitwise_and(place, 1)
    dataset_tag, first, core = lax.optimization_barrier(
        (dataset_tag, first.reshape(1), core.reshape(1))
    )

    sums = grouped_sums(
        node_feat,
        node_cot,
        edge_length,
        atom_count,
        edge_count,
        edge_source,
        edge_target,
        dataset_tag,
        charge_tag,
        spin_tag,
    )
    both = ("shard", "rep")
    planes = [[(16 * low + z) * reps + i for low in range(2) for i in range(reps)] for z in range(16)]
    columns = [[16 * low + z for z in range(16)] for low in range(2)]
    cores = [
        [(16 * low + z) * reps + 2 * i + core for i in range(8) for low in range(2)]
        for z in range(16)
        for core in range(2)
    ]
    sums = exchange(sums, both, planes)
    sums = jnp.sum(sums.astype(jnp.float32), axis=0).reshape(16, own, channels)
    sums = exchange(sums, "shard", columns)
    sums = jnp.sum(sums, axis=0)
    sums = exchange(jnp.broadcast_to(sums[None], (reps, own, channels)), "rep")
    grads, squares = expert_grads(
        dataset_gain, charge_gain, spin_gain, sums.reshape(8, 2, own, channels), shards
    )
    squares = exchange(squares, "shard")
    norm_limit = math.sqrt(experts * 2 * channels * channels)
    new_params, new_one, new_two, share = adam_update(
        first,
        squares,
        grads,
        params.reshape(rows),
        moment_one.reshape(rows),
        moment_two.reshape(rows),
        norm_limit,
    )
    share = exchange(share, "shard", columns).reshape(16, 2, own * 2, channels)
    share = jnp.broadcast_to(jnp.swapaxes(share, 0, 1)[None], (16, 2, 16, own * 2, channels))
    share = exchange(share, both, cores).reshape(8, 2, 2, 16, own * 2, channels)
    other = lax.ppermute(share, "rep", [(i, i ^ 1) for i in range(reps)])
    full_weights = place_half(1, core, other, place_half(0, core, share))
    full_weights = full_weights.reshape(experts, shards * own, 2, channels)
    return (new_params.reshape(shape), new_one.reshape(shape), new_two.reshape(shape), full_weights)


def solution(mesh):
    placed = (
        P(("shard", "rep"), None, None),
        P(("shard", "rep"), None, None),
        P(("shard", "rep"), None),
        P(("shard", "rep")),
        P(("shard", "rep")),
        P(("shard", "rep"), None),
        P(("shard", "rep"), None),
        P(("shard", "rep")),
        P(("shard", "rep")),
        P(("shard", "rep")),
        P(),
        P(),
        P(),
        P(None, "shard", None, None),
        P(None, "shard", None, None),
        P(None, "shard", None, None),
    )
    return jax.shard_map(
        local,
        mesh=mesh,
        in_specs=placed,
        out_specs=(
            P(None, "shard", None, None),
            P(None, "shard", None, None),
            P(None, "shard", None, None),
            P(),
        ),
        check_vma=False,
    )
```

```python
import functools
import math

import jax
import jax.numpy as jnp
from jax import lax
from jax.experimental import pallas as pl
from jax.experimental.pallas import tpu as pltpu
from jax.sharding import PartitionSpec as P

STEP = 10

beta_one = 0.9
beta_two = 0.999
adam_eps = 1e-08
learn_rate = 0.01
decay_rate = 0.01
cutoff_radius = 6.0

PARAMS = pltpu.CompilerParams(vmem_limit_bytes=24 * 2**20)


def envelope(length):
    ratio = length / cutoff_radius
    return 1.0 - 21.0 * ratio**5 + 35.0 * ratio**6 - 15.0 * ratio**7


def grouped_kernel(
    data_tag,
    charge_tag,
    spin_tag,
    atoms_ref,
    edges_ref,
    feat_ref,
    cot_ref,
    length_ref,
    source_ref,
    target_ref,
    out_ref,
    total,
):
    systems, atom_slots, width = feat_ref.shape
    channels = width // 2
    slots = length_ref.shape[1]
    total[...] = jnp.zeros_like(total)

    atom_ids = lax.broadcasted_iota(jnp.int32, (atom_slots, slots), 0)
    atom_ids = atom_ids.astype(jnp.float32).astype(jnp.bfloat16)
    zero = jnp.zeros((atom_slots, slots), jnp.bfloat16)
    one = jnp.ones((atom_slots, slots), jnp.bfloat16)
    system_ids = lax.broadcasted_iota(jnp.int32, (systems, slots), 0)
    slot_ids = lax.broadcasted_iota(jnp.int32, (systems, slots), 1)
    atoms = jnp.zeros((systems, slots), jnp.int32)
    edges = jnp.zeros((systems, slots), jnp.int32)
    for system in range(systems):
        atoms = jnp.where(system_ids == system, atoms_ref[system], atoms)
        edges = jnp.where(system_ids == system, edges_ref[system], edges)
    weight = envelope(length_ref[...]) * (float(atom_slots) / atoms.astype(jnp.float32))
    weight = jnp.where(slot_ids < edges, weight, 0.0).astype(jnp.bfloat16)
    source = source_ref[...].astype(jnp.float32).astype(jnp.bfloat16)
    target = target_ref[...].astype(jnp.float32).astype(jnp.bfloat16)

    links = []
    for system in range(systems):
        row = slice(system, system + 1)
        links.append(
            lax.dot_general(
                jnp.where(atom_ids == source[row], weight[row], zero),
                jnp.where(atom_ids == target[row], one, zero),
                (((1,), (1,)), ((), ())),
                preferred_element_type=jnp.float32,
            ).astype(jnp.bfloat16)
        )
    for system in range(systems):
        mixed = jnp.dot(links[system], cot_ref[system], preferred_element_type=jnp.float32)
        mixed = mixed.astype(jnp.bfloat16)
        swapped = jnp.concatenate([mixed[:, channels:], -mixed[:, :channels]], axis=1)
        feat = feat_ref[system]
        product = jnp.dot(
            jnp.concatenate([feat[:, :channels].T, feat[:, channels:].T], axis=1),
            jnp.concatenate([mixed, swapped], axis=0),
            preferred_element_type=jnp.float32,
        )
        tag = (data_tag[system] * 2 + charge_tag[system]) * 2 + spin_tag[system]
        total[2 * tag] += product[:, :channels]
        total[2 * tag + 1] += product[:, channels:]
    half = channels // 2
    for side in range(2):
        rows = pl.ds(side * half, half)
        out_ref[pl.ds(16 * side, 16)] = total[:, rows, :].astype(out_ref.dtype)


def grouped_sums(feat, cot, length, atoms, edges, source, target, data_tag, charge_tag, spin_tag):
    channels = feat.shape[2] // 2
    block = lambda shape: pl.BlockSpec(shape, lambda i: (0,) * len(shape))
    return pl.pallas_call(
        grouped_kernel,
        out_shape=jax.ShapeDtypeStruct((32, channels // 2, channels), jnp.bfloat16),
        grid=(1,),
        in_specs=[pl.BlockSpec(memory_space=pltpu.SMEM)] * 5
        + [block(array.shape) for array in (feat, cot, length, source, target)],
        out_specs=block((32, channels // 2, channels)),
        scratch_shapes=[pltpu.VMEM((16, channels, channels), jnp.float32)],
        name="grouped_sums",
    )(data_tag, charge_tag, spin_tag, atoms, edges, feat, cot, length, source, target)


def expert_kernel(
    first_ref,
    low_ref,
    data_ref,
    charge_ref,
    spin_ref,
    sums_ref,
    params_ref,
    one_ref,
    two_ref,
    grad_ref,
    share_ref,
    held,
):
    data_gain, charge_gain, spin_gain = data_ref[...], charge_ref[...], spin_ref[...]
    table = jnp.concatenate(
        [
            data_gain[d : d + 1] * charge_gain[c : c + 1] * spin_gain[s : s + 1]
            for d in range(2)
            for c in range(2)
            for s in range(2)
        ],
        axis=0,
    )
    mixing = table / jnp.sum(table, axis=1, keepdims=True)
    squares = None
    for low in range(2):
        for channel in range(4):
            for part in range(2):
                grad = lax.dot_general(
                    mixing,
                    sums_ref[low, :, part, channel, :],
                    (((0,), (0,)), ((), ())),
                    precision=lax.Precision.HIGHEST,
                    preferred_element_type=jnp.float32,
                )
                held[low, :, 2 * channel + part, :] = grad
                term = jnp.sum(grad * grad, axis=0, keepdims=True)
                squares = term if squares is None else squares + term
    grad_ref[...] = held[low_ref[0]]

    def rounded(value):
        return value.astype(jnp.bfloat16).astype(jnp.float32)

    pair = pl.ds(first_ref[0], 2)
    params = params_ref[pair].reshape(16, 128)
    upper = rounded(params)
    high = rounded(squares)
    middle = rounded(squares - high)
    share = jnp.concatenate(
        [
            held[low_ref[0], pair].reshape(16, 128),
            upper,
            params - upper,
            one_ref[pair].reshape(16, 128),
            two_ref[pair].reshape(16, 128),
            high,
            middle,
            squares - high - middle,
            jnp.zeros((5, 128), jnp.float32),
        ],
        axis=0,
    )
    share_ref[...] = jnp.broadcast_to(share.astype(jnp.bfloat16)[None], share_ref.shape)


def expert_grads(first, low, gains, sums, states):
    experts = gains[0].shape[1]
    vmem = pl.BlockSpec(memory_space=pltpu.VMEM)
    smem = pl.BlockSpec(memory_space=pltpu.SMEM)
    return pl.pallas_call(
        expert_kernel,
        out_shape=(
            jax.ShapeDtypeStruct((experts, 8, 128), jnp.float32),
            jax.ShapeDtypeStruct((16, 88, 128), jnp.bfloat16),
        ),
        in_specs=[smem, smem] + [vmem] * 7,
        out_specs=(vmem, vmem),
        scratch_shapes=[pltpu.VMEM((2, experts, 8, 128), jnp.float32)],
        compiler_params=PARAMS,
        name="expert_grads",
    )(first, low, *gains, sums, *states)


def adam_step(clipped, params, moment_one, moment_two):
    new_one = beta_one * moment_one + (1.0 - beta_one) * clipped
    new_two = beta_two * moment_two + (1.0 - beta_two) * clipped * clipped
    first_fix = 1.0 - beta_one**STEP
    second_fix = 1.0 - beta_two**STEP
    direction = new_one / first_fix / (jnp.sqrt(new_two / second_fix) + adam_eps)
    new_params = params - learn_rate * (direction + decay_rate * params)
    return (new_params, new_one, new_two)


def weight_kernel(norm_limit, share_ref, clip_ref, weight_ref):
    part = lambda row, count: share_ref[:, row : row + count, :].astype(jnp.float32)
    squares = jnp.sum(jnp.sum(part(80, 8), axis=0), axis=0, keepdims=True)
    square_sum = jnp.sum(squares, axis=1, keepdims=True)
    clip_factor = jnp.minimum(1.0, norm_limit / (jnp.sqrt(square_sum) + 1e-06))
    clip_ref[...] = jnp.broadcast_to(clip_factor, clip_ref.shape)
    for expert in range(2):
        row = 8 * expert
        weights = adam_step(
            clip_factor[None] * part(row, 8),
            part(16 + row, 8) + part(32 + row, 8),
            part(48 + row, 8),
            part(64 + row, 8),
        )[0].astype(jnp.bfloat16)
        for copy in range(weight_ref.shape[0]):
            weight_ref[copy, expert] = weights


def expert_weights(share, norm_limit):
    return pl.pallas_call(
        functools.partial(weight_kernel, norm_limit),
        out_shape=(
            jax.ShapeDtypeStruct((8, 128), jnp.float32),
            jax.ShapeDtypeStruct((16, 2, 16, 8, 128), jnp.bfloat16),
        ),
        compiler_params=PARAMS,
        name="expert_weights",
    )(share)


def adam_kernel(clip_ref, grad_ref, params_ref, one_ref, two_ref, *out_refs):
    states = (params_ref[...], one_ref[...], two_ref[...])
    for out_ref, value in zip(out_refs, adam_step(clip_ref[...] * grad_ref[...], *states)):
        out_ref[...] = value


def adam_update(clip, grads, states):
    size = 4 * grads.size
    return pl.pallas_call(
        adam_kernel,
        out_shape=(jax.ShapeDtypeStruct(grads.shape, jnp.float32),) * 3,
        compiler_params=PARAMS,
        cost_estimate=pl.CostEstimate(
            flops=20 * grads.size, transcendentals=grads.size, bytes_accessed=7 * size
        ),
        name="adam_update",
    )(clip, grads, *states)


def exchange(array, axis, groups=None):
    return lax.all_to_all(array, axis, 0, 0, axis_index_groups=groups, tiled=True)


def place_kernel(offset, core_ref, *refs):
    half_ref, out_ref, sems = refs[0], refs[-2], refs[-1]
    side = jnp.bitwise_xor(core_ref[0], offset)
    copies = [
        pltpu.make_async_copy(
            half_ref.at[:, low, expert], out_ref.at[side, :, expert, low], sems.at[2 * low + expert]
        )
        for low in range(2)
        for expert in range(2)
    ]
    for copy in copies:
        copy.start()
    for copy in copies:
        copy.wait()


def place_half(offset, core, half, *held):
    hbm = pl.BlockSpec(memory_space=pl.ANY)
    return pl.pallas_call(
        functools.partial(place_kernel, offset),
        out_shape=jax.ShapeDtypeStruct((2, 8, 2, 2) + half.shape[3:], half.dtype),
        in_specs=[
            pl.BlockSpec(memory_space=pltpu.SMEM),
            pl.BlockSpec(memory_space=pltpu.VMEM),
        ]
        + [hbm] * len(held),
        out_specs=hbm,
        scratch_shapes=[pltpu.SemaphoreType.DMA((4,))],
        input_output_aliases={2: 0} if held else {},
        compiler_params=PARAMS,
        cost_estimate=pl.CostEstimate(
            flops=0, transcendentals=0, bytes_accessed=2 * half.size * half.dtype.itemsize
        ),
        name="place_half",
    )(core, half, *held)


def local(
    node_feat,
    node_cot,
    edge_length,
    atom_count,
    edge_count,
    edge_source,
    edge_target,
    dataset_tag,
    charge_tag,
    spin_tag,
    dataset_gain,
    charge_gain,
    spin_gain,
    params,
    moment_one,
    moment_two,
):
    channels = node_feat.shape[2] // 2
    reps = 16
    experts, own = params.shape[:2]
    shape = params.shape
    rows = (experts, own * 2, channels)
    place = lax.axis_index("rep")
    core = jnp.bitwise_and(place, 1)
    first = core * (experts // 2) + jnp.bitwise_and(place, reps - 2)
    low = jnp.right_shift(lax.axis_index("shard"), 4)
    dataset_tag, first, core, low = lax.optimization_barrier(
        (dataset_tag, first.reshape(1), core.reshape(1), low.reshape(1))
    )
    states = tuple(array.reshape(rows) for array in (params, moment_one, moment_two))

    sums = grouped_sums(
        node_feat,
        node_cot,
        edge_length,
        atom_count,
        edge_count,
        edge_source,
        edge_target,
        dataset_tag,
        charge_tag,
        spin_tag,
    )
    both = ("shard", "rep")
    planes = [[(16 * low + z) * reps + i for low in range(2) for i in range(reps)] for z in range(16)]
    columns = [[16 * low + z for z in range(16)] for low in range(2)]
    cores = [
        [(16 * low + z) * reps + 2 * i + core for i in range(8) for low in range(2)]
        for z in range(16)
        for core in range(2)
    ]
    sums = exchange(sums, both, planes)
    sums = jnp.sum(sums.astype(jnp.float32), axis=0).reshape(16, own, channels)
    sums = exchange(sums, "shard", columns)
    sums = jnp.sum(sums, axis=0)
    sums = exchange(jnp.broadcast_to(sums[None], (2 * reps, own, channels)), both, planes)
    gains = (dataset_gain, charge_gain, spin_gain)
    grads, share = expert_grads(
        first, low, gains, sums.reshape(2, 8, 2, own, channels), states
    )
    share = exchange(share, "shard", columns)
    norm_limit = math.sqrt(experts * 2 * channels * channels)
    clip, share = expert_weights(share, norm_limit)
    share = exchange(share, both, cores).reshape(8, 2, 2, 16, own * 2, channels)
    clip, share = lax.optimization_barrier((clip, share))
    new_params, new_one, new_two = adam_update(clip, grads, states)
    other = lax.ppermute(share, "rep", [(i, i ^ 1) for i in range(reps)])
    full_weights = place_half(1, core, other, place_half(0, core, share))
    full_weights = full_weights.reshape(experts, 32 * own, 2, channels)
    return (new_params.reshape(shape), new_one.reshape(shape), new_two.reshape(shape), full_weights)


def solution(mesh):
    placed = (
        P(("shard", "rep"), None, None),
        P(("shard", "rep"), None, None),
        P(("shard", "rep"), None),
        P(("shard", "rep")),
        P(("shard", "rep")),
        P(("shard", "rep"), None),
        P(("shard", "rep"), None),
        P(("shard", "rep")),
        P(("shard", "rep")),
        P(("shard", "rep")),
        P(),
        P(),
        P(),
        P(None, "shard", None, None),
        P(None, "shard", None, None),
        P(None, "shard", None, None),
    )
    return jax.shard_map(
        local,
        mesh=mesh,
        in_specs=placed,
        out_specs=(
            P(None, "shard", None, None),
            P(None, "shard", None, None),
            P(None, "shard", None, None),
            P(),
        ),
        check_vma=False,
    )
```

```python
import functools
import math

import jax
import jax.numpy as jnp
from jax import lax
from jax.experimental import pallas as pl
from jax.experimental.pallas import tpu as pltpu
from jax.sharding import PartitionSpec as P

STEP = 10

beta_one = 0.9
beta_two = 0.999
adam_eps = 1e-08
learn_rate = 0.01
decay_rate = 0.01
cutoff_radius = 6.0

PARAMS = pltpu.CompilerParams(vmem_limit_bytes=24 * 2**20)


def envelope(length):
    ratio = length / cutoff_radius
    return 1.0 - 21.0 * ratio**5 + 35.0 * ratio**6 - 15.0 * ratio**7


def grouped_kernel(
    data_tag,
    charge_tag,
    spin_tag,
    atoms_ref,
    edges_ref,
    feat_ref,
    cot_ref,
    length_ref,
    source_ref,
    target_ref,
    out_ref,
    total,
):
    systems, atom_slots, width = feat_ref.shape
    channels = width // 2
    slots = length_ref.shape[1]
    total[...] = jnp.zeros_like(total)

    atom_ids = lax.broadcasted_iota(jnp.int32, (atom_slots, slots), 0)
    atom_ids = atom_ids.astype(jnp.float32).astype(jnp.bfloat16)
    zero = jnp.zeros((atom_slots, slots), jnp.bfloat16)
    one = jnp.ones((atom_slots, slots), jnp.bfloat16)
    system_ids = lax.broadcasted_iota(jnp.int32, (systems, slots), 0)
    slot_ids = lax.broadcasted_iota(jnp.int32, (systems, slots), 1)
    atoms = jnp.zeros((systems, slots), jnp.int32)
    edges = jnp.zeros((systems, slots), jnp.int32)
    for system in range(systems):
        atoms = jnp.where(system_ids == system, atoms_ref[system], atoms)
        edges = jnp.where(system_ids == system, edges_ref[system], edges)
    weight = envelope(length_ref[...]) * (float(atom_slots) / atoms.astype(jnp.float32))
    weight = jnp.where(slot_ids < edges, weight, 0.0).astype(jnp.bfloat16)
    source = source_ref[...].astype(jnp.float32).astype(jnp.bfloat16)
    target = target_ref[...].astype(jnp.float32).astype(jnp.bfloat16)

    links = []
    for system in range(systems):
        row = slice(system, system + 1)
        links.append(
            lax.dot_general(
                jnp.where(atom_ids == source[row], weight[row], zero),
                jnp.where(atom_ids == target[row], one, zero),
                (((1,), (1,)), ((), ())),
                preferred_element_type=jnp.float32,
            ).astype(jnp.bfloat16)
        )
    for system in range(systems):
        mixed = jnp.dot(links[system], cot_ref[system], preferred_element_type=jnp.float32)
        mixed = mixed.astype(jnp.bfloat16)
        swapped = jnp.concatenate([mixed[:, channels:], -mixed[:, :channels]], axis=1)
        feat = feat_ref[system]
        product = jnp.dot(
            jnp.concatenate([feat[:, :channels].T, feat[:, channels:].T], axis=1),
            jnp.concatenate([mixed, swapped], axis=0),
            preferred_element_type=jnp.float32,
        )
        tag = (data_tag[system] * 2 + charge_tag[system]) * 2 + spin_tag[system]
        total[2 * tag] += product[:, :channels]
        total[2 * tag + 1] += product[:, channels:]
    half = channels // 2
    for side in range(2):
        rows = pl.ds(side * half, half)
        out_ref[pl.ds(16 * side, 16)] = total[:, rows, :].astype(out_ref.dtype)


def grouped_sums(feat, cot, length, atoms, edges, source, target, data_tag, charge_tag, spin_tag):
    channels = feat.shape[2] // 2
    block = lambda shape: pl.BlockSpec(shape, lambda i: (0,) * len(shape))
    return pl.pallas_call(
        grouped_kernel,
        out_shape=jax.ShapeDtypeStruct((32, channels // 2, channels), jnp.bfloat16),
        grid=(1,),
        in_specs=[pl.BlockSpec(memory_space=pltpu.SMEM)] * 5
        + [block(array.shape) for array in (feat, cot, length, source, target)],
        out_specs=block((32, channels // 2, channels)),
        scratch_shapes=[pltpu.VMEM((16, channels, channels), jnp.float32)],
        name="grouped_sums",
    )(data_tag, charge_tag, spin_tag, atoms, edges, feat, cot, length, source, target)


def expert_kernel(
    first_ref,
    low_ref,
    data_ref,
    charge_ref,
    spin_ref,
    sums_ref,
    params_ref,
    one_ref,
    two_ref,
    grad_ref,
    share_ref,
    held,
):
    data_gain, charge_gain, spin_gain = data_ref[...], charge_ref[...], spin_ref[...]
    table = jnp.concatenate(
        [
            data_gain[d : d + 1] * charge_gain[c : c + 1] * spin_gain[s : s + 1]
            for d in range(2)
            for c in range(2)
            for s in range(2)
        ],
        axis=0,
    )
    mixing = table / jnp.sum(table, axis=1, keepdims=True)
    squares = None
    for low in range(2):
        for channel in range(4):
            for part in range(2):
                grad = lax.dot_general(
                    mixing,
                    sums_ref[low, :, part, channel, :],
                    (((0,), (0,)), ((), ())),
                    precision=lax.Precision.HIGHEST,
                    preferred_element_type=jnp.float32,
                )
                held[low, :, 2 * channel + part, :] = grad
                term = jnp.sum(grad * grad, axis=0, keepdims=True)
                squares = term if squares is None else squares + term
    grad_ref[...] = held[low_ref[0]]

    def rounded(value):
        return value.astype(jnp.bfloat16).astype(jnp.float32)

    pair = pl.ds(first_ref[0], 2)
    params = params_ref[pair].reshape(16, 128)
    upper = rounded(params)
    lower = params - upper
    square_sum = jnp.broadcast_to(jnp.sum(squares, axis=1, keepdims=True), lower.shape)
    high = rounded(square_sum)
    middle = rounded(square_sum - high)
    rows = lax.broadcasted_iota(jnp.int32, lower.shape, 0)
    lanes = lax.broadcasted_iota(jnp.int32, lower.shape, 1)
    terms = jnp.where(lanes == 2, square_sum - high - middle, 0.0)
    terms = jnp.where(lanes == 1, middle, terms)
    terms = jnp.where(lanes == 0, high, terms)
    share = jnp.concatenate(
        [
            held[low_ref[0], pair].reshape(16, 128),
            upper,
            jnp.where(rows == 15, terms, lower),
            one_ref[pair].reshape(16, 128),
            two_ref[pair].reshape(16, 128),
        ],
        axis=0,
    )
    share_ref[...] = jnp.broadcast_to(share.astype(jnp.bfloat16)[None], share_ref.shape)


def expert_grads(first, low, gains, sums, states):
    experts = gains[0].shape[1]
    vmem = pl.BlockSpec(memory_space=pltpu.VMEM)
    smem = pl.BlockSpec(memory_space=pltpu.SMEM)
    return pl.pallas_call(
        expert_kernel,
        out_shape=(
            jax.ShapeDtypeStruct((experts, 8, 128), jnp.float32),
            jax.ShapeDtypeStruct((16, 80, 128), jnp.bfloat16),
        ),
        in_specs=[smem, smem] + [vmem] * 7,
        out_specs=(vmem, vmem),
        scratch_shapes=[pltpu.VMEM((2, experts, 8, 128), jnp.float32)],
        compiler_params=PARAMS,
        name="expert_grads",
    )(first, low, *gains, sums, *states)


def adam_step(clipped, params, moment_one, moment_two):
    new_one = beta_one * moment_one + (1.0 - beta_one) * clipped
    new_two = beta_two * moment_two + (1.0 - beta_two) * clipped * clipped
    first_fix = 1.0 - beta_one**STEP
    second_fix = 1.0 - beta_two**STEP
    direction = new_one / first_fix / (jnp.sqrt(new_two / second_fix) + adam_eps)
    new_params = params - learn_rate * (direction + decay_rate * params)
    return (new_params, new_one, new_two)


def weight_kernel(norm_limit, share_ref, clip_ref, weight_ref):
    part = lambda row, count: share_ref[:, row : row + count, :].astype(jnp.float32)
    row_ids = lax.broadcasted_iota(jnp.int32, (16, 8, 128), 1)
    squares = jnp.sum(jnp.where(row_ids == 7, part(40, 8), 0.0), axis=0)
    square_sum = jnp.sum(jnp.sum(squares, axis=0, keepdims=True), axis=1, keepdims=True)
    clip_factor = jnp.minimum(1.0, norm_limit / (jnp.sqrt(square_sum) + 1e-06))
    clip_ref[...] = jnp.broadcast_to(clip_factor, clip_ref.shape)
    for expert in range(2):
        row = 8 * expert
        lower = part(32 + row, 8)
        if expert == 1:
            lower = jnp.where(row_ids == 7, 0.0, lower)
        weights = adam_step(
            clip_factor[None] * part(row, 8),
            part(16 + row, 8) + lower,
            part(48 + row, 8),
            part(64 + row, 8),
        )[0].astype(jnp.bfloat16)
        for copy in range(weight_ref.shape[0]):
            weight_ref[copy, expert] = weights


def expert_weights(share, norm_limit):
    return pl.pallas_call(
        functools.partial(weight_kernel, norm_limit),
        out_shape=(
            jax.ShapeDtypeStruct((8, 128), jnp.float32),
            jax.ShapeDtypeStruct((16, 2, 16, 8, 128), jnp.bfloat16),
        ),
        compiler_params=PARAMS,
        name="expert_weights",
    )(share)


def adam_kernel(clip_ref, grad_ref, params_ref, one_ref, two_ref, *out_refs):
    states = (params_ref[...], one_ref[...], two_ref[...])
    for out_ref, value in zip(out_refs, adam_step(clip_ref[...] * grad_ref[...], *states)):
        out_ref[...] = value


def adam_update(clip, grads, states):
    size = 4 * grads.size
    return pl.pallas_call(
        adam_kernel,
        out_shape=(jax.ShapeDtypeStruct(grads.shape, jnp.float32),) * 3,
        compiler_params=PARAMS,
        cost_estimate=pl.CostEstimate(
            flops=20 * grads.size, transcendentals=grads.size, bytes_accessed=7 * size
        ),
        name="adam_update",
    )(clip, grads, *states)


def exchange(array, axis, groups=None):
    return lax.all_to_all(array, axis, 0, 0, axis_index_groups=groups, tiled=True)


def place_kernel(offset, core_ref, *refs):
    half_ref, out_ref, sems = refs[0], refs[-2], refs[-1]
    side = jnp.bitwise_xor(core_ref[0], offset)
    copies = [
        pltpu.make_async_copy(
            half_ref.at[:, low, expert], out_ref.at[side, :, expert, low], sems.at[2 * low + expert]
        )
        for low in range(2)
        for expert in range(2)
    ]
    for copy in copies:
        copy.start()
    for copy in copies:
        copy.wait()


def place_half(offset, core, half, *held):
    hbm = pl.BlockSpec(memory_space=pl.ANY)
    return pl.pallas_call(
        functools.partial(place_kernel, offset),
        out_shape=jax.ShapeDtypeStruct((2, 8, 2, 2) + half.shape[3:], half.dtype),
        in_specs=[
            pl.BlockSpec(memory_space=pltpu.SMEM),
            pl.BlockSpec(memory_space=pltpu.VMEM),
        ]
        + [hbm] * len(held),
        out_specs=hbm,
        scratch_shapes=[pltpu.SemaphoreType.DMA((4,))],
        input_output_aliases={2: 0} if held else {},
        compiler_params=PARAMS,
        cost_estimate=pl.CostEstimate(
            flops=0, transcendentals=0, bytes_accessed=2 * half.size * half.dtype.itemsize
        ),
        name="place_half",
    )(core, half, *held)


def local(
    node_feat,
    node_cot,
    edge_length,
    atom_count,
    edge_count,
    edge_source,
    edge_target,
    dataset_tag,
    charge_tag,
    spin_tag,
    dataset_gain,
    charge_gain,
    spin_gain,
    params,
    moment_one,
    moment_two,
):
    channels = node_feat.shape[2] // 2
    reps = 16
    experts, own = params.shape[:2]
    shape = params.shape
    rows = (experts, own * 2, channels)
    place = lax.axis_index("rep")
    core = jnp.bitwise_and(place, 1)
    first = core * (experts // 2) + jnp.bitwise_and(place, reps - 2)
    low = jnp.right_shift(lax.axis_index("shard"), 4)
    dataset_tag, first, core, low = lax.optimization_barrier(
        (dataset_tag, first.reshape(1), core.reshape(1), low.reshape(1))
    )
    states = tuple(array.reshape(rows) for array in (params, moment_one, moment_two))

    sums = grouped_sums(
        node_feat,
        node_cot,
        edge_length,
        atom_count,
        edge_count,
        edge_source,
        edge_target,
        dataset_tag,
        charge_tag,
        spin_tag,
    )
    both = ("shard", "rep")
    planes = [[(16 * low + z) * reps + i for low in range(2) for i in range(reps)] for z in range(16)]
    columns = [[16 * low + z for z in range(16)] for low in range(2)]
    cores = [
        [(16 * low + z) * reps + 2 * i + core for i in range(8) for low in range(2)]
        for z in range(16)
        for core in range(2)
    ]
    sums = exchange(sums, both, planes)
    sums = jnp.sum(sums.astype(jnp.float32), axis=0).reshape(16, own, channels)
    sums = exchange(sums, "shard", columns)
    sums = jnp.sum(sums, axis=0)
    sums = exchange(jnp.broadcast_to(sums[None], (2 * reps, own, channels)), both, planes)
    gains = (dataset_gain, charge_gain, spin_gain)
    grads, share = expert_grads(
        first, low, gains, sums.reshape(2, 8, 2, own, channels), states
    )
    share = exchange(share, "shard", columns)
    norm_limit = math.sqrt(experts * 2 * channels * channels)
    clip, share = expert_weights(share, norm_limit)
    share = exchange(share, both, cores).reshape(8, 2, 2, 16, own * 2, channels)
    clip, share = lax.optimization_barrier((clip, share))
    new_params, new_one, new_two = adam_update(clip, grads, states)
    other = lax.ppermute(share, "rep", [(i, i ^ 1) for i in range(reps)])
    full_weights = place_half(1, core, other, place_half(0, core, share))
    full_weights = full_weights.reshape(experts, 32 * own, 2, channels)
    return (new_params.reshape(shape), new_one.reshape(shape), new_two.reshape(shape), full_weights)


def solution(mesh):
    placed = (
        P(("shard", "rep"), None, None),
        P(("shard", "rep"), None, None),
        P(("shard", "rep"), None),
        P(("shard", "rep")),
        P(("shard", "rep")),
        P(("shard", "rep"), None),
        P(("shard", "rep"), None),
        P(("shard", "rep")),
        P(("shard", "rep")),
        P(("shard", "rep")),
        P(),
        P(),
        P(),
        P(None, "shard", None, None),
        P(None, "shard", None, None),
        P(None, "shard", None, None),
    )
    return jax.shard_map(
        local,
        mesh=mesh,
        in_specs=placed,
        out_specs=(
            P(None, "shard", None, None),
            P(None, "shard", None, None),
            P(None, "shard", None, None),
            P(),
        ),
        check_vma=False,
    )
```

```python
import functools
import math

import jax
import jax.numpy as jnp
from jax import lax
from jax.experimental import pallas as pl
from jax.experimental.pallas import tpu as pltpu
from jax.sharding import PartitionSpec as P

STEP = 10

beta_one = 0.9
beta_two = 0.999
adam_eps = 1e-08
learn_rate = 0.01
decay_rate = 0.01
cutoff_radius = 6.0

PARAMS = pltpu.CompilerParams(vmem_limit_bytes=24 * 2**20)


def envelope(length):
    ratio = length / cutoff_radius
    return 1.0 - 21.0 * ratio**5 + 35.0 * ratio**6 - 15.0 * ratio**7


def grouped_kernel(
    data_tag,
    charge_tag,
    spin_tag,
    atoms_ref,
    edges_ref,
    feat_ref,
    cot_ref,
    length_ref,
    source_ref,
    target_ref,
    out_ref,
    total,
):
    systems, atom_slots, width = feat_ref.shape
    channels = width // 2
    slots = length_ref.shape[1]
    total[...] = jnp.zeros_like(total)

    atom_ids = lax.broadcasted_iota(jnp.int32, (atom_slots, slots), 0)
    atom_ids = atom_ids.astype(jnp.float32).astype(jnp.bfloat16)
    zero = jnp.zeros((atom_slots, slots), jnp.bfloat16)
    one = jnp.ones((atom_slots, slots), jnp.bfloat16)
    system_ids = lax.broadcasted_iota(jnp.int32, (systems, slots), 0)
    slot_ids = lax.broadcasted_iota(jnp.int32, (systems, slots), 1)
    atoms = jnp.zeros((systems, slots), jnp.int32)
    edges = jnp.zeros((systems, slots), jnp.int32)
    for system in range(systems):
        atoms = jnp.where(system_ids == system, atoms_ref[system], atoms)
        edges = jnp.where(system_ids == system, edges_ref[system], edges)
    weight = envelope(length_ref[...]) * (float(atom_slots) / atoms.astype(jnp.float32))
    weight = jnp.where(slot_ids < edges, weight, 0.0).astype(jnp.bfloat16)
    source = source_ref[...].astype(jnp.float32).astype(jnp.bfloat16)
    target = target_ref[...].astype(jnp.float32).astype(jnp.bfloat16)

    links = []
    for system in range(systems):
        row = slice(system, system + 1)
        links.append(
            lax.dot_general(
                jnp.where(atom_ids == source[row], weight[row], zero),
                jnp.where(atom_ids == target[row], one, zero),
                (((1,), (1,)), ((), ())),
                preferred_element_type=jnp.float32,
            ).astype(jnp.bfloat16)
        )
    for system in range(systems):
        mixed = jnp.dot(links[system], cot_ref[system], preferred_element_type=jnp.float32)
        mixed = mixed.astype(jnp.bfloat16)
        swapped = jnp.concatenate([mixed[:, channels:], -mixed[:, :channels]], axis=1)
        feat = feat_ref[system]
        product = jnp.dot(
            jnp.concatenate([feat[:, :channels].T, feat[:, channels:].T], axis=1),
            jnp.concatenate([mixed, swapped], axis=0),
            preferred_element_type=jnp.float32,
        )
        tag = (data_tag[system] * 2 + charge_tag[system]) * 2 + spin_tag[system]
        total[2 * tag] += product[:, :channels]
        total[2 * tag + 1] += product[:, channels:]
    half = channels // 2
    for side in range(2):
        rows = pl.ds(side * half, half)
        out_ref[pl.ds(16 * side, 16)] = total[:, rows, :].astype(out_ref.dtype)


def grouped_sums(feat, cot, length, atoms, edges, source, target, data_tag, charge_tag, spin_tag):
    channels = feat.shape[2] // 2
    block = lambda shape: pl.BlockSpec(shape, lambda i: (0,) * len(shape))
    return pl.pallas_call(
        grouped_kernel,
        out_shape=jax.ShapeDtypeStruct((32, channels // 2, channels), jnp.bfloat16),
        grid=(1,),
        in_specs=[pl.BlockSpec(memory_space=pltpu.SMEM)] * 5
        + [block(array.shape) for array in (feat, cot, length, source, target)],
        out_specs=block((32, channels // 2, channels)),
        scratch_shapes=[pltpu.VMEM((16, channels, channels), jnp.float32)],
        name="grouped_sums",
    )(data_tag, charge_tag, spin_tag, atoms, edges, feat, cot, length, source, target)


def rounded(value):
    return value.astype(jnp.bfloat16).astype(jnp.float32)


def scatter_kernel(first_ref, sums_ref, params_ref, out_ref):
    total = jnp.sum(sums_ref[...].astype(jnp.float32), axis=0)
    high = rounded(total)
    params = params_ref[pl.ds(first_ref[0], 1)]
    lower = jnp.broadcast_to(params - rounded(params), (16, 8, 128))
    parts = [high.reshape(16, 4, 128), (total - high).reshape(16, 4, 128), lower]
    out_ref[...] = jnp.concatenate(parts, axis=1).astype(jnp.bfloat16)


def scatter_message(first, sums, params):
    vmem = pl.BlockSpec(memory_space=pltpu.VMEM)
    return pl.pallas_call(
        scatter_kernel,
        out_shape=jax.ShapeDtypeStruct((16, 16, 128), jnp.bfloat16),
        in_specs=[pl.BlockSpec(memory_space=pltpu.SMEM), vmem, vmem],
        out_specs=vmem,
        compiler_params=PARAMS,
        name="scatter_message",
    )(first, sums, params)


def expert_kernel(
    first_ref,
    low_ref,
    data_ref,
    charge_ref,
    spin_ref,
    sums_ref,
    params_ref,
    one_ref,
    two_ref,
    grad_ref,
    share_ref,
    held,
):
    data_gain, charge_gain, spin_gain = data_ref[...], charge_ref[...], spin_ref[...]
    table = jnp.concatenate(
        [
            data_gain[d : d + 1] * charge_gain[c : c + 1] * spin_gain[s : s + 1]
            for d in range(2)
            for c in range(2)
            for s in range(2)
        ],
        axis=0,
    )
    mixing = table / jnp.sum(table, axis=1, keepdims=True)
    squares = None
    for low in range(2):
        for channel in range(4):
            for part in range(2):
                grad = lax.dot_general(
                    mixing,
                    sums_ref[low, :, part, channel, :],
                    (((0,), (0,)), ((), ())),
                    precision=lax.Precision.HIGHEST,
                    preferred_element_type=jnp.float32,
                )
                held[low, :, 2 * channel + part, :] = grad
                term = jnp.sum(grad * grad, axis=0, keepdims=True)
                squares = term if squares is None else squares + term
    grad_ref[...] = held[low_ref[0]]

    pair = pl.ds(first_ref[0], 2)
    params = params_ref[pair].reshape(16, 128)
    upper = rounded(params)
    lower = params - upper
    square_sum = jnp.broadcast_to(jnp.sum(squares, axis=1, keepdims=True), lower.shape)
    high = rounded(square_sum)
    middle = rounded(square_sum - high)
    rows = lax.broadcasted_iota(jnp.int32, lower.shape, 0)
    lanes = lax.broadcasted_iota(jnp.int32, lower.shape, 1)
    terms = jnp.where(lanes == 2, square_sum - high - middle, 0.0)
    terms = jnp.where(lanes == 1, middle, terms)
    terms = jnp.where(lanes == 0, high, terms)
    share = jnp.concatenate(
        [
            held[low_ref[0], pair].reshape(16, 128),
            upper,
            jnp.where(rows == 15, terms, lower)[8:],
            one_ref[pair].reshape(16, 128),
            two_ref[pair].reshape(16, 128),
        ],
        axis=0,
    )
    share_ref[...] = jnp.broadcast_to(share.astype(jnp.bfloat16)[None], share_ref.shape)


def expert_grads(first, low, gains, sums, states):
    experts = gains[0].shape[1]
    vmem = pl.BlockSpec(memory_space=pltpu.VMEM)
    smem = pl.BlockSpec(memory_space=pltpu.SMEM)
    return pl.pallas_call(
        expert_kernel,
        out_shape=(
            jax.ShapeDtypeStruct((experts, 8, 128), jnp.float32),
            jax.ShapeDtypeStruct((16, 72, 128), jnp.bfloat16),
        ),
        in_specs=[smem, smem] + [vmem] * 7,
        out_specs=(vmem, vmem),
        scratch_shapes=[pltpu.VMEM((2, experts, 8, 128), jnp.float32)],
        compiler_params=PARAMS,
        name="expert_grads",
    )(first, low, *gains, sums, *states)


def adam_step(clipped, params, moment_one, moment_two):
    new_one = beta_one * moment_one + (1.0 - beta_one) * clipped
    new_two = beta_two * moment_two + (1.0 - beta_two) * clipped * clipped
    first_fix = 1.0 - beta_one**STEP
    second_fix = 1.0 - beta_two**STEP
    direction = new_one / first_fix / (jnp.sqrt(new_two / second_fix) + adam_eps)
    new_params = params - learn_rate * (direction + decay_rate * params)
    return (new_params, new_one, new_two)


def weight_kernel(norm_limit, share_ref, early_ref, clip_ref, weight_ref):
    part = lambda row, count: share_ref[:, row : row + count, :].astype(jnp.float32)
    row_ids = lax.broadcasted_iota(jnp.int32, (16, 8, 128), 1)
    squares = jnp.sum(jnp.where(row_ids == 7, part(32, 8), 0.0), axis=0)
    square_sum = jnp.sum(jnp.sum(squares, axis=0, keepdims=True), axis=1, keepdims=True)
    clip_factor = jnp.minimum(1.0, norm_limit / (jnp.sqrt(square_sum) + 1e-06))
    clip_ref[...] = jnp.broadcast_to(clip_factor, clip_ref.shape)
    for expert in range(2):
        row = 8 * expert
        if expert == 0:
            lower = early_ref[:, 8:16, :].astype(jnp.float32)
        else:
            lower = jnp.where(row_ids == 7, 0.0, part(32, 8))
        weights = adam_step(
            clip_factor[None] * part(row, 8),
            part(16 + row, 8) + lower,
            part(40 + row, 8),
            part(56 + row, 8),
        )[0].astype(jnp.bfloat16)
        for copy in range(weight_ref.shape[0]):
            weight_ref[copy, expert] = weights


def expert_weights(share, early, norm_limit):
    return pl.pallas_call(
        functools.partial(weight_kernel, norm_limit),
        out_shape=(
            jax.ShapeDtypeStruct((8, 128), jnp.float32),
            jax.ShapeDtypeStruct((16, 2, 16, 8, 128), jnp.bfloat16),
        ),
        compiler_params=PARAMS,
        name="expert_weights",
    )(share, early)


def adam_kernel(clip_ref, grad_ref, params_ref, one_ref, two_ref, *out_refs):
    states = (params_ref[...], one_ref[...], two_ref[...])
    for out_ref, value in zip(out_refs, adam_step(clip_ref[...] * grad_ref[...], *states)):
        out_ref[...] = value


def adam_update(clip, grads, states):
    size = 4 * grads.size
    return pl.pallas_call(
        adam_kernel,
        out_shape=(jax.ShapeDtypeStruct(grads.shape, jnp.float32),) * 3,
        compiler_params=PARAMS,
        cost_estimate=pl.CostEstimate(
            flops=20 * grads.size, transcendentals=grads.size, bytes_accessed=7 * size
        ),
        name="adam_update",
    )(clip, grads, *states)


def exchange(array, axis, groups=None):
    return lax.all_to_all(array, axis, 0, 0, axis_index_groups=groups, tiled=True)


def place_kernel(offset, core_ref, *refs):
    half_ref, out_ref, sems = refs[0], refs[-2], refs[-1]
    side = jnp.bitwise_xor(core_ref[0], offset)
    copies = [
        pltpu.make_async_copy(
            half_ref.at[:, low, expert], out_ref.at[side, :, expert, low], sems.at[2 * low + expert]
        )
        for low in range(2)
        for expert in range(2)
    ]
    for copy in copies:
        copy.start()
    for copy in copies:
        copy.wait()


def place_half(offset, core, half, *held):
    hbm = pl.BlockSpec(memory_space=pl.ANY)
    return pl.pallas_call(
        functools.partial(place_kernel, offset),
        out_shape=jax.ShapeDtypeStruct((2, 8, 2, 2) + half.shape[3:], half.dtype),
        in_specs=[
            pl.BlockSpec(memory_space=pltpu.SMEM),
            pl.BlockSpec(memory_space=pltpu.VMEM),
        ]
        + [hbm] * len(held),
        out_specs=hbm,
        scratch_shapes=[pltpu.SemaphoreType.DMA((4,))],
        input_output_aliases={2: 0} if held else {},
        compiler_params=PARAMS,
        cost_estimate=pl.CostEstimate(
            flops=0, transcendentals=0, bytes_accessed=2 * half.size * half.dtype.itemsize
        ),
        name="place_half",
    )(core, half, *held)


def local(
    node_feat,
    node_cot,
    edge_length,
    atom_count,
    edge_count,
    edge_source,
    edge_target,
    dataset_tag,
    charge_tag,
    spin_tag,
    dataset_gain,
    charge_gain,
    spin_gain,
    params,
    moment_one,
    moment_two,
):
    channels = node_feat.shape[2] // 2
    reps = 16
    experts, own = params.shape[:2]
    shape = params.shape
    rows = (experts, own * 2, channels)
    place = lax.axis_index("rep")
    core = jnp.bitwise_and(place, 1)
    first = core * (experts // 2) + jnp.bitwise_and(place, reps - 2)
    low = jnp.right_shift(lax.axis_index("shard"), 4)
    dataset_tag, first, core, low = lax.optimization_barrier(
        (dataset_tag, first.reshape(1), core.reshape(1), low.reshape(1))
    )
    states = tuple(array.reshape(rows) for array in (params, moment_one, moment_two))

    sums = grouped_sums(
        node_feat,
        node_cot,
        edge_length,
        atom_count,
        edge_count,
        edge_source,
        edge_target,
        dataset_tag,
        charge_tag,
        spin_tag,
    )
    both = ("shard", "rep")
    planes = [[(16 * low + z) * reps + i for low in range(2) for i in range(reps)] for z in range(16)]
    columns = [[16 * low + z for z in range(16)] for low in range(2)]
    cores = [
        [(16 * low + z) * reps + 2 * i + core for i in range(8) for low in range(2)]
        for z in range(16)
        for core in range(2)
    ]
    sums = exchange(sums, both, planes)
    early = exchange(scatter_message(first, sums, states[0]), "shard", columns)
    sums = jnp.sum(early[:, : 2 * own].astype(jnp.float32), axis=0)
    sums = sums[:own] + sums[own:]
    sums = exchange(jnp.broadcast_to(sums[None], (2 * reps, own, channels)), both, planes)
    gains = (dataset_gain, charge_gain, spin_gain)
    grads, share = expert_grads(
        first, low, gains, sums.reshape(2, 8, 2, own, channels), states
    )
    share = exchange(share, "shard", columns)
    norm_limit = math.sqrt(experts * 2 * channels * channels)
    clip, share = expert_weights(share, early, norm_limit)
    share = exchange(share, both, cores).reshape(8, 2, 2, 16, own * 2, channels)
    clip, share = lax.optimization_barrier((clip, share))
    new_params, new_one, new_two = adam_update(clip, grads, states)
    other = lax.ppermute(share, "rep", [(i, i ^ 1) for i in range(reps)])
    full_weights = place_half(1, core, other, place_half(0, core, share))
    full_weights = full_weights.reshape(experts, 32 * own, 2, channels)
    return (new_params.reshape(shape), new_one.reshape(shape), new_two.reshape(shape), full_weights)


def solution(mesh):
    placed = (
        P(("shard", "rep"), None, None),
        P(("shard", "rep"), None, None),
        P(("shard", "rep"), None),
        P(("shard", "rep")),
        P(("shard", "rep")),
        P(("shard", "rep"), None),
        P(("shard", "rep"), None),
        P(("shard", "rep")),
        P(("shard", "rep")),
        P(("shard", "rep")),
        P(),
        P(),
        P(),
        P(None, "shard", None, None),
        P(None, "shard", None, None),
        P(None, "shard", None, None),
    )
    return jax.shard_map(
        local,
        mesh=mesh,
        in_specs=placed,
        out_specs=(
            P(None, "shard", None, None),
            P(None, "shard", None, None),
            P(None, "shard", None, None),
            P(),
        ),
        check_vma=False,
    )
```

```python
import functools
import math

import jax
import jax.numpy as jnp
from jax import lax
from jax.experimental import pallas as pl
from jax.experimental.pallas import tpu as pltpu
from jax.sharding import PartitionSpec as P

STEP = 10

beta_one = 0.9
beta_two = 0.999
adam_eps = 1e-08
learn_rate = 0.01
decay_rate = 0.01
cutoff_radius = 6.0

PARAMS = pltpu.CompilerParams(vmem_limit_bytes=24 * 2**20)


def envelope(length):
    ratio = length / cutoff_radius
    return 1.0 - 21.0 * ratio**5 + 35.0 * ratio**6 - 15.0 * ratio**7


def grouped_kernel(
    data_tag,
    charge_tag,
    spin_tag,
    atoms_ref,
    edges_ref,
    feat_ref,
    cot_ref,
    length_ref,
    source_ref,
    target_ref,
    out_ref,
    total,
):
    systems, atom_slots, width = feat_ref.shape
    channels = width // 2
    slots = length_ref.shape[1]
    total[...] = jnp.zeros_like(total)

    atom_ids = lax.broadcasted_iota(jnp.int32, (atom_slots, slots), 0)
    atom_ids = atom_ids.astype(jnp.float32).astype(jnp.bfloat16)
    zero = jnp.zeros((atom_slots, slots), jnp.bfloat16)
    one = jnp.ones((atom_slots, slots), jnp.bfloat16)
    system_ids = lax.broadcasted_iota(jnp.int32, (systems, slots), 0)
    slot_ids = lax.broadcasted_iota(jnp.int32, (systems, slots), 1)
    atoms = jnp.zeros((systems, slots), jnp.int32)
    edges = jnp.zeros((systems, slots), jnp.int32)
    for system in range(systems):
        atoms = jnp.where(system_ids == system, atoms_ref[system], atoms)
        edges = jnp.where(system_ids == system, edges_ref[system], edges)
    weight = envelope(length_ref[...]) * (float(atom_slots) / atoms.astype(jnp.float32))
    weight = jnp.where(slot_ids < edges, weight, 0.0).astype(jnp.bfloat16)
    source = source_ref[...].astype(jnp.float32).astype(jnp.bfloat16)
    target = target_ref[...].astype(jnp.float32).astype(jnp.bfloat16)

    links = []
    for system in range(systems):
        row = slice(system, system + 1)
        links.append(
            lax.dot_general(
                jnp.where(atom_ids == source[row], weight[row], zero),
                jnp.where(atom_ids == target[row], one, zero),
                (((1,), (1,)), ((), ())),
                preferred_element_type=jnp.float32,
            ).astype(jnp.bfloat16)
        )
    for system in range(systems):
        mixed = jnp.dot(links[system], cot_ref[system], preferred_element_type=jnp.float32)
        mixed = mixed.astype(jnp.bfloat16)
        swapped = jnp.concatenate([mixed[:, channels:], -mixed[:, :channels]], axis=1)
        feat = feat_ref[system]
        product = jnp.dot(
            jnp.concatenate([feat[:, :channels].T, feat[:, channels:].T], axis=1),
            jnp.concatenate([mixed, swapped], axis=0),
            preferred_element_type=jnp.float32,
        )
        tag = (data_tag[system] * 2 + charge_tag[system]) * 2 + spin_tag[system]
        total[2 * tag] += product[:, :channels]
        total[2 * tag + 1] += product[:, channels:]
    half = channels // 2
    for side in range(2):
        rows = pl.ds(side * half, half)
        out_ref[pl.ds(16 * side, 16)] = total[:, rows, :].astype(out_ref.dtype)


def grouped_sums(feat, cot, length, atoms, edges, source, target, data_tag, charge_tag, spin_tag):
    channels = feat.shape[2] // 2
    block = lambda shape: pl.BlockSpec(shape, lambda i: (0,) * len(shape))
    return pl.pallas_call(
        grouped_kernel,
        out_shape=jax.ShapeDtypeStruct((32, channels // 2, channels), jnp.bfloat16),
        grid=(1,),
        in_specs=[pl.BlockSpec(memory_space=pltpu.SMEM)] * 5
        + [block(array.shape) for array in (feat, cot, length, source, target)],
        out_specs=block((32, channels // 2, channels)),
        scratch_shapes=[pltpu.VMEM((16, channels, channels), jnp.float32)],
        name="grouped_sums",
    )(data_tag, charge_tag, spin_tag, atoms, edges, feat, cot, length, source, target)


def rounded(value):
    return value.astype(jnp.bfloat16).astype(jnp.float32)


def scatter_kernel(first_ref, sums_ref, params_ref, out_ref):
    total = jnp.sum(sums_ref[...].astype(jnp.float32), axis=0)
    high = rounded(total)
    params = params_ref[pl.ds(first_ref[0], 1)]
    lower = jnp.broadcast_to(params - rounded(params), (16, 8, 128))
    parts = [high.reshape(16, 4, 128), (total - high).reshape(16, 4, 128), lower]
    out_ref[...] = jnp.concatenate(parts, axis=1).astype(jnp.bfloat16)


def scatter_message(first, sums, params):
    vmem = pl.BlockSpec(memory_space=pltpu.VMEM)
    return pl.pallas_call(
        scatter_kernel,
        out_shape=jax.ShapeDtypeStruct((16, 16, 128), jnp.bfloat16),
        in_specs=[pl.BlockSpec(memory_space=pltpu.SMEM), vmem, vmem],
        out_specs=vmem,
        compiler_params=PARAMS,
        name="scatter_message",
    )(first, sums, params)


def expert_kernel(
    first_ref,
    low_ref,
    data_ref,
    charge_ref,
    spin_ref,
    sums_ref,
    params_ref,
    one_ref,
    two_ref,
    grad_ref,
    share_ref,
    held,
):
    data_gain, charge_gain, spin_gain = data_ref[...], charge_ref[...], spin_ref[...]
    table = jnp.concatenate(
        [
            data_gain[d : d + 1] * charge_gain[c : c + 1] * spin_gain[s : s + 1]
            for d in range(2)
            for c in range(2)
            for s in range(2)
        ],
        axis=0,
    )
    mixing = table / jnp.sum(table, axis=1, keepdims=True)
    squares = None
    for low in range(2):
        for channel in range(4):
            for part in range(2):
                grad = lax.dot_general(
                    mixing,
                    sums_ref[low, :, part, channel, :],
                    (((0,), (0,)), ((), ())),
                    precision=lax.Precision.HIGHEST,
                    preferred_element_type=jnp.float32,
                )
                held[low, :, 2 * channel + part, :] = grad
                term = jnp.sum(grad * grad, axis=0, keepdims=True)
                squares = term if squares is None else squares + term
    grad_ref[...] = held[low_ref[0]]

    pair = pl.ds(first_ref[0], 2)
    params = params_ref[pair].reshape(16, 128)
    upper = rounded(params)
    lower = params - upper
    square_sum = jnp.broadcast_to(jnp.sum(squares, axis=1, keepdims=True), lower.shape)
    high = rounded(square_sum)
    middle = rounded(square_sum - high)
    rows = lax.broadcasted_iota(jnp.int32, lower.shape, 0)
    lanes = lax.broadcasted_iota(jnp.int32, lower.shape, 1)
    terms = jnp.where(lanes == 2, square_sum - high - middle, 0.0)
    terms = jnp.where(lanes == 1, middle, terms)
    terms = jnp.where(lanes == 0, high, terms)
    share = jnp.concatenate(
        [
            held[low_ref[0], pair].reshape(16, 128),
            upper,
            jnp.where(rows == 15, terms, lower)[8:],
            one_ref[pair].reshape(16, 128),
            two_ref[pair].reshape(16, 128),
        ],
        axis=0,
    )
    share_ref[...] = jnp.broadcast_to(share.astype(jnp.bfloat16)[None], share_ref.shape)


def expert_grads(first, low, gains, sums, states):
    experts = gains[0].shape[1]
    vmem = pl.BlockSpec(memory_space=pltpu.VMEM)
    smem = pl.BlockSpec(memory_space=pltpu.SMEM)
    return pl.pallas_call(
        expert_kernel,
        out_shape=(
            jax.ShapeDtypeStruct((experts, 8, 128), jnp.float32),
            jax.ShapeDtypeStruct((16, 72, 128), jnp.bfloat16),
        ),
        in_specs=[smem, smem] + [vmem] * 7,
        out_specs=(vmem, vmem),
        scratch_shapes=[pltpu.VMEM((2, experts, 8, 128), jnp.float32)],
        compiler_params=PARAMS,
        name="expert_grads",
    )(first, low, *gains, sums, *states)


def adam_step(clipped, params, moment_one, moment_two):
    new_one = beta_one * moment_one + (1.0 - beta_one) * clipped
    new_two = beta_two * moment_two + (1.0 - beta_two) * clipped * clipped
    first_fix = 1.0 - beta_one**STEP
    second_fix = 1.0 - beta_two**STEP
    direction = new_one / first_fix / (jnp.sqrt(new_two / second_fix) + adam_eps)
    new_params = params - learn_rate * (direction + decay_rate * params)
    return (new_params, new_one, new_two)


def weight_kernel(norm_limit, share_ref, early_ref, clip_ref, weight_ref):
    part = lambda row, count: share_ref[:, row : row + count, :].astype(jnp.float32)
    row_ids = lax.broadcasted_iota(jnp.int32, (16, 8, 128), 1)
    squares = jnp.sum(jnp.where(row_ids == 7, part(32, 8), 0.0), axis=0)
    square_sum = jnp.sum(jnp.sum(squares, axis=0, keepdims=True), axis=1, keepdims=True)
    clip_factor = jnp.minimum(1.0, norm_limit / (jnp.sqrt(square_sum) + 1e-06))
    clip_ref[...] = jnp.broadcast_to(clip_factor, clip_ref.shape)
    for expert in range(2):
        row = 8 * expert
        if expert == 0:
            lower = early_ref[:, 8:16, :].astype(jnp.float32)
        else:
            lower = jnp.where(row_ids == 7, 0.0, part(32, 8))
        weights = adam_step(
            clip_factor[None] * part(row, 8),
            part(16 + row, 8) + lower,
            part(40 + row, 8),
            part(56 + row, 8),
        )[0].astype(jnp.bfloat16)
        for copy in range(weight_ref.shape[0]):
            weight_ref[copy, expert] = weights


def expert_weights(share, early, norm_limit):
    return pl.pallas_call(
        functools.partial(weight_kernel, norm_limit),
        out_shape=(
            jax.ShapeDtypeStruct((8, 128), jnp.float32),
            jax.ShapeDtypeStruct((16, 2, 16, 8, 128), jnp.bfloat16),
        ),
        compiler_params=PARAMS,
        name="expert_weights",
    )(share, early)


def adam_kernel(clip_ref, grad_ref, params_ref, one_ref, two_ref, *out_refs):
    states = (params_ref[...], one_ref[...], two_ref[...])
    for out_ref, value in zip(out_refs, adam_step(clip_ref[...] * grad_ref[...], *states)):
        out_ref[...] = value


def adam_update(clip, grads, states):
    size = 4 * grads.size
    return pl.pallas_call(
        adam_kernel,
        out_shape=(jax.ShapeDtypeStruct(grads.shape, jnp.float32),) * 3,
        compiler_params=PARAMS,
        cost_estimate=pl.CostEstimate(
            flops=20 * grads.size, transcendentals=grads.size, bytes_accessed=7 * size
        ),
        name="adam_update",
    )(clip, grads, *states)


def exchange(array, axis, groups=None):
    return lax.all_to_all(array, axis, 0, 0, axis_index_groups=groups, tiled=True)


def place_kernel(offset, core_ref, *refs):
    half_ref, out_ref, sems = refs[0], refs[-2], refs[-1]
    side = jnp.bitwise_xor(core_ref[0], offset)
    copies = [
        pltpu.make_async_copy(
            half_ref.at[low, :, expert], out_ref.at[side, :, expert, low], sems.at[2 * low + expert]
        )
        for low in range(2)
        for expert in range(2)
    ]
    for copy in copies:
        copy.start()
    for copy in copies:
        copy.wait()


def place_half(offset, core, half, *held):
    hbm = pl.BlockSpec(memory_space=pl.ANY)
    return pl.pallas_call(
        functools.partial(place_kernel, offset),
        out_shape=jax.ShapeDtypeStruct((2, 8, 2, 2) + half.shape[3:], half.dtype),
        in_specs=[
            pl.BlockSpec(memory_space=pltpu.SMEM),
            pl.BlockSpec(memory_space=pltpu.VMEM),
        ]
        + [hbm] * len(held),
        out_specs=hbm,
        scratch_shapes=[pltpu.SemaphoreType.DMA((4,))],
        input_output_aliases={2: 0} if held else {},
        compiler_params=PARAMS,
        cost_estimate=pl.CostEstimate(
            flops=0, transcendentals=0, bytes_accessed=2 * half.size * half.dtype.itemsize
        ),
        name="place_half",
    )(core, half, *held)


def local(
    node_feat,
    node_cot,
    edge_length,
    atom_count,
    edge_count,
    edge_source,
    edge_target,
    dataset_tag,
    charge_tag,
    spin_tag,
    dataset_gain,
    charge_gain,
    spin_gain,
    params,
    moment_one,
    moment_two,
):
    channels = node_feat.shape[2] // 2
    reps = 16
    experts, own = params.shape[:2]
    shape = params.shape
    rows = (experts, own * 2, channels)
    place = lax.axis_index("rep")
    core = jnp.bitwise_and(place, 1)
    first = core * (experts // 2) + jnp.bitwise_and(place, reps - 2)
    low = jnp.right_shift(lax.axis_index("shard"), 4)
    dataset_tag, first, core, low = lax.optimization_barrier(
        (dataset_tag, first.reshape(1), core.reshape(1), low.reshape(1))
    )
    states = tuple(array.reshape(rows) for array in (params, moment_one, moment_two))

    sums = grouped_sums(
        node_feat,
        node_cot,
        edge_length,
        atom_count,
        edge_count,
        edge_source,
        edge_target,
        dataset_tag,
        charge_tag,
        spin_tag,
    )
    both = ("shard", "rep")
    planes = [[(16 * low + z) * reps + i for low in range(2) for i in range(reps)] for z in range(16)]
    columns = [[16 * low + z for z in range(16)] for low in range(2)]
    cores = [
        [(16 * low + z) * reps + 2 * i + core for low in range(2) for i in range(8)]
        for z in range(16)
        for core in range(2)
    ]
    sums = exchange(sums, both, planes)
    early = exchange(scatter_message(first, sums, states[0]), "shard", columns)
    sums = jnp.sum(early[:, : 2 * own].astype(jnp.float32), axis=0)
    sums = sums[:own] + sums[own:]
    sums = exchange(jnp.broadcast_to(sums[None], (2 * reps, own, channels)), both, planes)
    gains = (dataset_gain, charge_gain, spin_gain)
    grads, share = expert_grads(
        first, low, gains, sums.reshape(2, 8, 2, own, channels), states
    )
    share = exchange(share, "shard", columns)
    norm_limit = math.sqrt(experts * 2 * channels * channels)
    clip, share = expert_weights(share, early, norm_limit)
    share = exchange(share, both, cores).reshape(2, 8, 2, 16, own * 2, channels)
    clip, share = lax.optimization_barrier((clip, share))
    new_params, new_one, new_two = adam_update(clip, grads, states)
    other = lax.ppermute(share, "rep", [(i, i ^ 1) for i in range(reps)])
    full_weights = place_half(1, core, other, place_half(0, core, share))
    full_weights = full_weights.reshape(experts, 32 * own, 2, channels)
    return (new_params.reshape(shape), new_one.reshape(shape), new_two.reshape(shape), full_weights)


def solution(mesh):
    placed = (
        P(("shard", "rep"), None, None),
        P(("shard", "rep"), None, None),
        P(("shard", "rep"), None),
        P(("shard", "rep")),
        P(("shard", "rep")),
        P(("shard", "rep"), None),
        P(("shard", "rep"), None),
        P(("shard", "rep")),
        P(("shard", "rep")),
        P(("shard", "rep")),
        P(),
        P(),
        P(),
        P(None, "shard", None, None),
        P(None, "shard", None, None),
        P(None, "shard", None, None),
    )
    return jax.shard_map(
        local,
        mesh=mesh,
        in_specs=placed,
        out_specs=(
            P(None, "shard", None, None),
            P(None, "shard", None, None),
            P(None, "shard", None, None),
            P(),
        ),
        check_vma=False,
    )
```
